768 devices in a mesh: sec: 128 (over x, z_lo, y), blk: 6 (over z_hi, core).
Axes of the slice: x: 4, y: 8, z: 12 (z_hi: 3, z_lo: 4; z = z_hi * 4 + z_lo), core: 2. Of those that a mesh axis runs over, the one named last changes fastest.
Arguments:
- slab_state: float32 [9, 8, 2048, 768], P(None, None, 'sec', 'blk'), may hold values from -6 to 6
- buoyancy: float32 [8, 2048, 768], P(None, 'sec', 'blk'), may hold values from 0.5 to 1
- lame_lambda: float32 [8, 2048, 768], P(None, 'sec', 'blk'), may hold values from 0.5 to 2
- lame_mu: float32 [8, 2048, 768], P(None, 'sec', 'blk'), may hold values from 0.3 to 1.2
- face_map: int32 [768], replicated, may hold values from 0 to 3071
- band_widths: int32 [128, 6], P('sec'), may hold values from 2 to 9
- ocean_state: float32 [3, 2048, 3072], P(None, 'sec', 'blk'), may hold values from -6 to 6
- water_depth: float32 [2048, 3072], P('sec', 'blk'), may hold values from 0.25 to 1
Outputs:
- slab_out: float32 [9, 8, 2048, 768], P(None, None, 'sec', 'blk')
- ocean_out: float32 [3, 2048, 3072], P(None, 'sec', 'blk')
The draws below stay inside these ranges and needn't reach their ends.
Inputs may be any that keep to these rules, and one draw needn't show every extreme that they name: `face_map`: each entry is the ocean column over which that seafloor face column lies. `band_widths`: the Kajiura band width of each ocean tile in ocean cells.
All inputs are finite; a program needn't handle non-finite values.
Results may differ from the reference program's by a relative error of at most 0.00014.
Values sent between devices are 32-bit elements; how exact they have to be, the bound alone decides.
No kernel may reach another device: no remote copies, remote signals or barrier semaphores. Data moves between devices by JAX's collectives and lax.ppermute only.
A program may use at most 64 MiB of HBM per device.

```python
import math
import jax
import jax.numpy as jnp
import numpy as np
from jax import lax

THICKNESS = 8
STRIKE_DEV = 16
OCEAN_DEV = 512
FIELDS = 9
SLAB_STEPS = 2
WAVE_STEPS = 4
STRIKE = 2048
DIP = 768
OCEAN_COLS = 3072
TILE_ROWS = 128
TILE_COLS = 6
N_SEC = 128


def touch_ends(result, own_key, smallest, top_value):
    longest = result.shape.index(max(result.shape))
    spots = []
    for shift in (0, 1):
        where = [jax.random.randint(jax.random.fold_in(own_key, axis), (), 0, length) for axis, length in enumerate(result.shape)]
        where[longest] = (where[longest] + shift) % result.shape[longest]
        spots.append(tuple(where))
    return result.at[spots[0]].set(smallest).at[spots[1]].set(top_value)


def block_scale(stream_key, dims, pieces, low, largest):
    def one(axis_at, parts):
        draws = jax.random.uniform(jax.random.fold_in(jax.random.fold_in(stream_key, 6), axis_at), (parts,), jnp.float32, low / len(pieces), largest / len(pieces))
        return jnp.repeat(jnp.exp(draws), dims[axis_at] // parts).reshape((-1,) + (1,) * (len(dims) - axis_at - 1))

    gain = one(*pieces[0])
    for cut in pieces[1:]:
        gain = gain * one(*cut)
    return gain


def rank_table(amount, skew):
    loads = [(1 << 20) // math.isqrt(rank ** skew) + 1 for rank in range(1, amount + 1)]
    width = 1 + sum(loads) // (1 << 30)
    return np.cumsum(np.array([max(1, weight // width) for weight in loads]))


def ranked_ids(rng, shape, amount, skew):
    listing = rank_table(amount, skew)
    ticket = jax.random.randint(jax.random.fold_in(rng, 1), shape, 0, int(listing[amount - 1]))
    rank = jnp.searchsorted(jnp.asarray(listing, jnp.int32), ticket, side="right")
    return jax.random.permutation(jax.random.fold_in(rng, 2), amount)[rank].astype(jnp.int32)


def gaussian(stream_key, dims, deviation, limit, pieces=(), kind=jnp.bfloat16):
    gain = block_scale(stream_key, dims, pieces, -0.22, 0.18) if pieces else 1.0
    values = jax.random.normal(stream_key, dims, jnp.float32) * deviation * gain
    return jnp.minimum(jnp.maximum(values, -limit), limit).astype(kind)


def setup_inputs(seed: int = 0) -> dict:
    streams_of = jax.random.split(jax.random.key(seed), 9)
    slab_state = gaussian(streams_of[0], (FIELDS, THICKNESS, STRIKE, DIP), 1.0, 6.0, ((2, 128), (3, 6)), jnp.float32)
    buoyancy = jnp.clip(jnp.exp(math.log(1.0) - 0.6931472 * jax.random.uniform(streams_of[1], (THICKNESS, STRIKE, DIP), jnp.float32) ** block_scale(streams_of[1], (THICKNESS, STRIKE, DIP), ((1, 128), (2, 6)), -0.2, 0.2)), 0.5, 1.0)
    lame_lambda = jnp.clip(jnp.exp(math.log(2.0) - 1.3862944 * jax.random.uniform(streams_of[2], (THICKNESS, STRIKE, DIP), jnp.float32) ** block_scale(streams_of[2], (THICKNESS, STRIKE, DIP), ((1, 128), (2, 6)), -0.2, 0.2)), 0.5, 2.0)
    lame_mu = jnp.clip(jnp.exp(math.log(1.2) - 1.3862944 * jax.random.uniform(streams_of[3], (THICKNESS, STRIKE, DIP), jnp.float32) ** block_scale(streams_of[3], (THICKNESS, STRIKE, DIP), ((1, 128), (2, 6)), -0.2, 0.2)), 0.3, 1.2)
    face_map = touch_ends(ranked_ids(streams_of[4], (DIP,), OCEAN_COLS, 2), jax.random.fold_in(streams_of[4], 3), 0, OCEAN_COLS - 1).astype(jnp.int32)
    band_widths = touch_ends(jax.random.randint(streams_of[5], (TILE_ROWS, TILE_COLS), 2, 10), jax.random.fold_in(streams_of[5], 1), 2, 9).astype(jnp.int32)
    ocean_state = gaussian(streams_of[6], (3, STRIKE, OCEAN_COLS), 1.0, 6.0, ((1, 128), (2, 6)), jnp.float32)
    water_depth = jnp.clip(jnp.exp(math.log(1.0) - 1.3862944 * jax.random.uniform(streams_of[7], (STRIKE, OCEAN_COLS), jnp.float32) ** block_scale(streams_of[7], (STRIKE, OCEAN_COLS), ((0, 128), (1, 6)), -0.2, 0.2)), 0.25, 1.0)
    return {"slab_state": slab_state, "buoyancy": buoyancy, "lame_lambda": lame_lambda, "lame_mu": lame_mu, "face_map": face_map, "band_widths": band_widths, "ocean_state": ocean_state, "water_depth": water_depth}


time_step = 0.25
wave_step = 0.5


def sech_kernel(distance, band_width):
    scaled = jnp.abs(distance) * (math.pi / 2.0) / band_width
    decay = jnp.exp(-scaled)
    return 2.0 * decay / (1.0 + decay * decay) / (2.0 * band_width)


def offset_slice(values, dimension, offset):
    slicer = [slice(1, -1)] * 3
    extent = values.shape[dimension]
    slicer[dimension] = slice(1 + offset, extent - 1 + offset)
    return values[tuple(slicer)]


def forward(values, dimension):
    return offset_slice(values, dimension, 1) - offset_slice(values, dimension, 0)


def backward(values, dimension):
    return offset_slice(values, dimension, 0) - offset_slice(values, dimension, -1)


def new_velocity(velocity, stress_padded, buoyancy):
    results = []
    for dimension in range(3):
        summed = forward(stress_padded[dimension], dimension)
        for across in range(3):
            if across != dimension:
                summed = summed + backward(stress_padded[6 - dimension - across], across)
        results.append(velocity[dimension] + time_step * buoyancy * summed)
    return jnp.stack(results)


def new_stress(stress, velocity_padded, lame_lambda, lame_mu):
    strain_rates = [backward(velocity_padded[dimension], dimension) for dimension in range(3)]
    dilatation = strain_rates[0] + strain_rates[1] + strain_rates[2]
    results = []
    for dimension in range(3):
        results.append(stress[dimension] + time_step * (lame_lambda * dilatation + 2.0 * lame_mu * strain_rates[dimension]))
    results.append(stress[3] + time_step * lame_mu * (forward(velocity_padded[1], 2) + forward(velocity_padded[2], 1)))
    results.append(stress[4] + time_step * lame_mu * (forward(velocity_padded[0], 2) + forward(velocity_padded[2], 0)))
    results.append(stress[5] + time_step * lame_mu * (forward(velocity_padded[0], 1) + forward(velocity_padded[1], 0)))
    return jnp.stack(results)


def pad_all(values):
    return jnp.pad(values, ((0, 0), (1, 1), (1, 1), (1, 1)))


def reference(slab_state, buoyancy, lame_lambda, lame_mu, face_map, band_widths, ocean_state, water_depth):
    velocity = slab_state[:3]
    stress = slab_state[3:]
    surface_rate = jnp.zeros(slab_state.shape[2:], jnp.float32)
    for stepping in range(SLAB_STEPS):
        velocity = new_velocity(velocity, pad_all(stress), buoyancy)
        surface_rate = surface_rate + velocity[0, 0]
        stress = new_stress(stress, pad_all(velocity), lame_lambda, lame_mu)
    slab_out = jnp.concatenate([velocity, stress], 0)
    uplift = time_step * surface_rate
    columns = jnp.arange(OCEAN_COLS, dtype=jnp.int32)

    def section_source(section):
        strip_rows = lax.dynamic_slice_in_dim(uplift, section * STRIKE_DEV, STRIKE_DEV, 0)
        tile_bands = lax.dynamic_index_in_dim(band_widths, section, 0, keepdims=False)
        widths = jnp.repeat(tile_bands, OCEAN_DEV).astype(jnp.float32)
        distance = (columns[:, None] - face_map[None, :]).astype(jnp.float32)
        kernel = sech_kernel(distance, widths[:, None])
        return jnp.einsum("xy,cy->xc", strip_rows, kernel, precision=lax.Precision.HIGHEST)

    source = lax.map(section_source, jnp.arange(N_SEC, dtype=jnp.int32)).reshape(STRIKE, OCEAN_COLS)
    surface = ocean_state[0] + source
    flux_strike = ocean_state[1]
    flux_dip = ocean_state[2]
    for stepping in range(WAVE_STEPS):
        padded_strike = jnp.pad(flux_strike, 1)
        padded_dip = jnp.pad(flux_dip, 1)
        surface = surface - wave_step * 0.5 * ((padded_strike[2:, 1:-1] - padded_strike[:-2, 1:-1]) + (padded_dip[1:-1, 2:] - padded_dip[1:-1, :-2]))
        padded_surface = jnp.pad(surface, 1)
        flux_strike = flux_strike - wave_step * 0.5 * water_depth * (padded_surface[2:, 1:-1] - padded_surface[:-2, 1:-1])
        flux_dip = flux_dip - wave_step * 0.5 * water_depth * (padded_surface[1:-1, 2:] - padded_surface[1:-1, :-2])
    ocean_out = jnp.stack([surface, flux_strike, flux_dip])
    return slab_out, ocean_out
```

```python
import math

import jax
import jax.numpy as jnp
from jax import lax
from jax.experimental import pallas as pl
from jax.experimental.pallas import tpu as pltpu
from jax.sharding import PartitionSpec as P

Q = 0.25
R = 16
LANES = 128
DEPTH = 8
COLS = 512
S11, S22, S33, S23, S13, S12, BUO, LAM, MU = 3, 4, 5, 6, 7, 8, 9, 10, 11
UP_PLANES = [(S11, 0), (S11, 1), (S11, 2)] + [
    (f, t) for f in (S12, S13, S23, S22, S33, 0, 1, 2, BUO, LAM, MU) for t in (0, 1)
]
N_UP = len(UP_PLANES)
UP_INDEX = {ft: i for i, ft in enumerate(UP_PLANES)}
STRIP = N_UP
N_STRIP = 24
MISC = STRIP + N_STRIP
OCEAN = MISC + 1
SEC_TILES = OCEAN + 16
B_UP, B_FACTOR, B_SLAB, B_OCEAN, BLK_TILES = 0, 4, 6, 12, 13
F32 = jnp.float32
BF16 = jnp.bfloat16
VMEM = pl.BlockSpec(memory_space=pltpu.VMEM)


def lane_iota(shape):
    return lax.broadcasted_iota(jnp.int32, shape, len(shape) - 1)


def row_iota(shape):
    return lax.broadcasted_iota(jnp.int32, shape, 0)


def reader(slab, mats):
    def read(f, t, rows):
        return slab[f, t, rows, :] if f < 9 else mats[f - 9][t, rows, :]

    return read


def pack_kernel(slab, buo, lam, mu, ocean, depth, widths, first, second):
    odd = lax.rem(lax.axis_index("sec"), 2)
    read = reader(slab, (buo, lam, mu))
    for out, lower in ((first, odd), (second, 1 - odd)):
        start = pl.multiple_of(lower * 8, 8)
        rows = pl.ds(start, 8)
        for i, (f, t) in enumerate(UP_PLANES):
            out[i] = read(f, t, rows)
        for p in range(96):
            f, t = p // 8, p % 8
            strip = jnp.where(lower == 1, read(f, t, slice(14, 16)), read(f, t, slice(0, 2)))
            out[STRIP + p // 4, 2 * (p % 4) : 2 * (p % 4) + 2, :] = strip
        out[MISC] = jnp.zeros((8, LANES), F32)
        for t in (0, 1):
            out[MISC, t : t + 1, :] = read(S12, t, slice(7, 8))
        out[MISC, 2:3, 0 : widths.shape[1]] = widths[...].astype(F32)
        for f in range(4):
            for k in range(4):
                cols = slice(k * LANES, (k + 1) * LANES)
                out[OCEAN + 4 * f + k] = ocean[f, rows, cols] if f < 3 else depth[rows, cols]


def sides(first, second):
    odd = lax.rem(lax.axis_index("sec"), 2)

    def top(i):
        return jnp.where(odd == 0, first[i], second[i])

    def bottom(i):
        return jnp.where(odd == 0, second[i], first[i])

    return top, bottom


def uplift_kernel(slab, buo, lam, mu, ocean, depth, first, second, send, strips):
    me = lax.axis_index("blk")
    read = reader(slab, (buo, lam, mu))
    top, bottom = sides(first, second)
    shape = (32, LANES)
    lane, row = lane_iota(shape), row_iota(shape)

    def plane(f, t):
        i = UP_INDEX[(f, t)]
        return jnp.concatenate([top(i), read(f, t, slice(0, 16)), bottom(i)], axis=0)

    def north(x):
        return pltpu.roll(x, 1, 0)

    def south(x):
        return pltpu.roll(x, 31, 0)

    def west(x):
        return jnp.where(lane == 0, 0.0, pltpu.roll(x, 1, 1))

    def east(x):
        return jnp.where(lane == LANES - 1, 0.0, pltpu.roll(x, LANES - 1, 1))

    s11 = [plane(S11, t) for t in range(3)]
    s22, s33, s23, s13, s12 = ([plane(f, t) for t in (0, 1)] for f in (S22, S33, S23, S13, S12))
    b, la, m = ([plane(f, t) for t in (0, 1)] for f in (BUO, LAM, MU))
    misc = top(MISC)
    v1, v2, v3 = [], [], []
    for t in (0, 1):
        above = lambda s: s[t] - s[t - 1] if t else s[t]
        s12n = jnp.where(row == 0, misc[t : t + 1, :], north(s12[t]))
        v1.append(plane(0, t) + Q * b[t] * (s11[t + 1] - s11[t] + (s12[t] - s12n) + (s13[t] - west(s13[t]))))
        v2.append(plane(1, t) + Q * b[t] * (south(s22[t]) - s22[t] + above(s12) + (s23[t] - west(s23[t]))))
        v3.append(plane(2, t) + Q * b[t] * (east(s33[t]) - s33[t] + above(s13) + (s23[t] - north(s23[t]))))
    n11 = []
    for t in (0, 1):
        d1 = v1[t] - v1[t - 1] if t else v1[t]
        dil = d1 + (v2[t] - north(v2[t])) + (v3[t] - west(v3[t]))
        n11.append(s11[t] + Q * (la[t] * dil + 2.0 * m[t] * d1))
    n12 = s12[0] + Q * m[0] * (south(v1[0]) - v1[0] + v2[1] - v2[0])
    n13 = s13[0] + Q * m[0] * (east(v1[0]) - v1[0] + v3[1] - v3[0])
    g = Q * Q * b[0]
    rise = 2.0 * Q * v1[0] + g * (n11[1] - n11[0] + n12 - north(n12) + n13 - west(n13))

    la0, la1 = Q * la[0], Q * la[1]
    m0, m1 = la0 + 2.0 * Q * m[0], la1 + 2.0 * Q * m[1]
    q0 = Q * m[0]
    q0n = north(q0)
    b0, b1 = Q * b[0], Q * b[1]
    left = [
        g * (la1 + q0) * b1,
        -g * (la0 + q0) * b0,
        g * q0,
        g * q0 * s13[0],
        s13[0],
        south(s13[0]),
        north(s13[0]),
        s13[1],
        s23[0],
        north(s23[0]),
        s23[1],
        north(s23[1]),
        v3[1],
        b1,
        v3[0],
        b0,
        n13,
        q0,
        q0 * s13[0],
        q0 * b1,
        q0 * b0,
        s13[0],
    ]
    right = [
        s33[1],
        s33[0],
        v1[0],
        -b0,
        -(2.0 * Q - g * (m1 + m0 + 2.0 * q0 + q0n)) * b0,
        -g * q0 * south(b0),
        -g * q0n * north(b0),
        -g * m1 * b1,
        g * (la0 + q0) * b0,
        -g * (la0 + q0n) * north(b0),
        -g * (la1 + q0) * b1,
        g * (la1 + q0n) * north(b1),
        -g * la1,
        -g * la1 * s33[1],
        g * la0,
        g * la0 * s33[0],
        -g,
        -g * v1[0],
        g * b0,
        -g * s33[1],
        g * s33[0],
        -pltpu.roll(g, LANES - 1, 1) * q0 * b0,
    ]
    factors = jnp.zeros(shape, F32)
    for i, (x, y) in enumerate(zip(left, right)):
        factors = jnp.where(lane == i, pltpu.roll(x, (i + 1) % LANES, 1), factors)
        factors = jnp.where(lane == 32 + i, pltpu.roll(y, 32 + i, 1), factors)
    packed = jnp.where(lane[:16] < 64, factors[:16], pltpu.roll(factors[16:], 64, 1))

    tile = (8, LANES)
    tlane = lane_iota(tile)
    strips[...] = jnp.zeros((96, 8, LANES), F32)
    odd = lax.rem(lax.axis_index("sec"), 2)
    for p in range(96):
        i, at = STRIP + p // 4, slice(2 * (p % 4), 2 * (p % 4) + 2)
        a, c = first[i, at, :], second[i, at, :]
        strips[p, 0:2, :] = jnp.where(odd == 0, c, a)
        strips[p, 6:8, :] = jnp.where(odd == 0, a, c)
    heads, tails = [], []
    for r in range(3):
        for half in range(2):
            head, tail = jnp.zeros(tile, F32), jnp.zeros(tile, F32)
            for t in range(4 * half, 4 * half + 4):
                for f in range(12):
                    at = 24 * (t % 4) + 2 * f
                    x = read(f, t, slice(8 * r, 8 * r + 8)) if r < 2 else strips[f * 8 + t]
                    x = pltpu.roll(x, at + 2, 1)
                    tail = jnp.where((tlane >= at) & (tlane < at + 2), x, tail)
                    head = jnp.where((tlane >= at + 2) & (tlane < at + 4), x, head)
            heads.append(head)
            tails.append(tail)
    head, tail = jnp.zeros(tile, F32), jnp.zeros(tile, F32)
    for f in range(4):
        for r in range(4):
            at = 32 * f + 8 * r
            ends = []
            for k in (0, 3):
                cols = slice(k * LANES, (k + 1) * LANES)
                rows = slice(8 * r - 8, 8 * r)
                if r == 0:
                    x = top(OCEAN + 4 * f + k)
                elif r == 3:
                    x = bottom(OCEAN + 4 * f + k)
                else:
                    x = ocean[f, rows, cols] if f < 3 else depth[rows, cols]
                ends.append(x)
            here = (tlane >= at) & (tlane < at + 8)
            head = jnp.where(here, pltpu.roll(ends[0], at, 1), head)
            tail = jnp.where(here, pltpu.roll(ends[1], (at + 8) % LANES, 1), tail)
    heads.append(head)
    tails.append(tail)
    for d in range(send.shape[0]):
        for r in range(4):
            send[d, B_UP + r] = rise[8 * r : 8 * r + 8]
        for r in range(2):
            send[d, B_FACTOR + r] = packed[8 * r : 8 * r + 8]
        for i in range(7):
            send[d, B_SLAB + i] = jnp.where(d < me, heads[i], tails[i])


def filter_kernel(face, widths, first, second, hi, lo):
    me = lax.axis_index("blk")
    top, bottom = sides(first, second)
    lane = lane_iota((1, LANES))
    face_at = (face[...] - me * COLS).astype(F32)
    width = face.shape[1]

    def scales(row):
        out = []
        for j in (me, me + 1, me - 1):
            w = jnp.sum(jnp.where(lane[:, : row.shape[1]] == j, row, 0.0), axis=1, keepdims=True)
            w = jnp.where(w > 0.0, w, 1.0)
            out.append((-(math.pi / 2.0) * math.log2(math.e) / w, 1.0 / w))
        return out

    groups = [scales(top(MISC)[2:3, :]), scales(widths[...].astype(F32)), scales(bottom(MISC)[2:3, :])]

    def put(k, rows, distance, rate, gain):
        decay = jnp.exp2(distance * rate)
        value = decay / (1.0 + decay * decay) * gain
        upper = value.astype(BF16)
        hi[k, rows, :] = upper
        lo[k, rows, :] = (value - upper.astype(F32)).astype(BF16)

    @pl.loop(0, COLS // 16)
    def _(c):
        start = pl.multiple_of(c * 16, 16)
        at = (lax.broadcasted_iota(jnp.int32, (16, width), 0) + start).astype(F32)
        distance = jnp.abs(at - face_at)
        for k in range(3):
            put(k, pl.ds(start, 16), distance, *groups[k][0])

    row = row_iota((16, width))
    at = jnp.where(row < 8, row + COLS, row - 16).astype(F32)
    distance = jnp.abs(at - face_at)
    for k in range(3):
        rate = jnp.where(row < 8, groups[k][1][0], groups[k][2][0])
        gain = jnp.where(row < 8, groups[k][1][1], groups[k][2][1])
        put(k, slice(COLS, COLS + 16), distance, rate, gain)


def final_kernel(
    slab, buo, lam, mu, ocean, depth, first, second, strips, recv, hi, lo, slab_out, ocean_out, cells, mats, flat
):
    sec, me = lax.axis_index("sec"), lax.axis_index("blk")
    n_sec, n_blk = lax.axis_size("sec"), lax.axis_size("blk")
    read = reader(slab, (buo, lam, mu))
    top, bottom = sides(first, second)
    shape = (32, LANES)
    lane = lane_iota(shape)
    before, after = jnp.maximum(me - 1, 0), jnp.minimum(me + 1, n_blk - 1)
    tile = (8, LANES)
    tlane = lane_iota(tile)

    rises = [jnp.concatenate([recv[j, B_UP + r] for r in range(4)], axis=0) for j in range(n_blk)]
    factors = []
    for j in range(n_blk):
        x = jnp.concatenate([recv[j, B_FACTOR], recv[j, B_FACTOR + 1]], axis=0)
        factors.append(jnp.concatenate([x, pltpu.roll(x, 64, 1)], axis=0))
    for j in range(n_blk - 1):
        terms = factors[j] * pltpu.roll(factors[j + 1], LANES - 32, 1)
        pick = lambda a, z: jnp.sum(jnp.where((lane >= a) & (lane < z), terms, 0.0), axis=1, keepdims=True)
        rises[j] = rises[j] + jnp.where(lane == LANES - 1, pick(0, 4), 0.0)
        rises[j + 1] = rises[j + 1] + jnp.where(lane == 0, pick(4, 21), 0.0) + jnp.where(lane == 1, pick(21, 22), 0.0)
    rise = jnp.concatenate(rises, axis=1)
    rise_hi = rise.astype(BF16)
    rise_lo = (rise - rise_hi.astype(F32)).astype(BF16)

    def dot(a, c):
        return lax.dot_general(a, c, (((1,), (1,)), ((), ())), preferred_element_type=F32)

    source = None
    col = lane_iota((COLS + 16, 32))
    for k in range(3):
        a = hi[k]
        part = dot(a, rise_hi) + dot(a, rise_lo) + dot(lo[k], rise_hi)
        source = part if k == 0 else jnp.where(col >= (0, 8, 24)[k], part, source)
    flat[...] = jnp.zeros((5 * LANES, LANES), F32)
    flat[0 : COLS + 8, 0:32] = source[0 : COLS + 8]
    flat[5 * LANES - 8 : 5 * LANES, 0:32] = source[COLS + 8 : COLS + 16]
    source = jnp.concatenate(
        [flat[k * LANES : (k + 1) * LANES, :].T[0:32] for k in range(5)], axis=1
    )

    ring = (32, 5 * LANES)
    seas = []
    for f in range(4):
        tiles = []
        for k in range(4):
            cols = slice(k * LANES, (k + 1) * LANES)
            own = ocean[f, :, cols] if f < 3 else depth[:, cols]
            i = OCEAN + 4 * f + k
            tiles.append(jnp.concatenate([top(i), own, bottom(i)], axis=0))
        halo = []
        for r in range(4):
            at = 32 * f + 8 * r
            east_in = pltpu.roll(recv[after, B_OCEAN], (LANES - at) % LANES, 1)
            west_in = pltpu.roll(recv[before, B_OCEAN], (2 * LANES - 8 - at) % LANES, 1)
            x = jnp.where((tlane < 8) & (me < n_blk - 1), east_in, 0.0)
            halo.append(jnp.where((tlane >= LANES - 8) & (me > 0), west_in, x))
        tiles.append(jnp.concatenate(halo, axis=0))
        seas.append(jnp.concatenate(tiles, axis=1))
    surface, strike, dip, water = seas
    at = lane_iota(ring)
    at = jnp.where(at >= 5 * LANES - 8, at - 5 * LANES, at)
    x, y = row_iota(ring) - 8 + sec * R, at + me * COLS
    wet = (x >= 0) & (x < n_sec * R) & (y >= 0) & (y < n_blk * COLS) & (at < COLS + 8)
    surface = surface + source
    water = 0.25 * water
    for step in range(4):
        change = pltpu.roll(strike, 31, 0) - pltpu.roll(strike, 1, 0)
        change = change + (pltpu.roll(dip, 5 * LANES - 1, 1) - pltpu.roll(dip, 1, 1))
        surface = jnp.where(wet, surface - 0.25 * change, 0.0)
        strike = strike - water * (pltpu.roll(surface, 31, 0) - pltpu.roll(surface, 1, 0))
        dip = dip - water * (pltpu.roll(surface, 5 * LANES - 1, 1) - pltpu.roll(surface, 1, 1))
    ocean_out[0] = surface[8:24, 0:COLS]
    ocean_out[1] = strike[8:24, 0:COLS]
    ocean_out[2] = dip[8:24, 0:COLS]

    for f in range(9):
        for t in (0, DEPTH + 1):
            cells[f, t] = jnp.zeros((24, 2 * LANES), F32)
    west_on, east_on = me > 0, me < n_blk - 1
    for r in range(3):
        rows = slice(8 * r, 8 * r + 8)
        for half in range(2):
            i = B_SLAB + 2 * r + half
            east_in = jnp.where(east_on, recv[after, i], 0.0)
            west_in = jnp.where(west_on, recv[before, i], 0.0)
            for t in range(4 * half, 4 * half + 4):
                for f in range(12):
                    at = 24 * (t % 4) + 2 * f
                    edge = jnp.where(tlane < at + 2, west_in, east_in)
                    edge = pltpu.roll(edge, LANES - at - 2, 1)
                    own = read(f, t, rows) if r < 2 else strips[f * 8 + t]
                    if f < 9:
                        cells[f, t + 1, rows, 0:LANES] = own
                        cells[f, t + 1, rows, LANES:] = edge
                    else:
                        mats[f - 9, t, rows, 0:LANES] = own
                        mats[f - 9, t, rows, LANES:] = edge

    north = lambda v: pltpu.roll(v, 1, 0)
    south = lambda v: pltpu.roll(v, 23, 0)
    west = lambda v: pltpu.roll(v, 1, 1)
    east = lambda v: pltpu.roll(v, 2 * LANES - 1, 1)
    for step in range(2):

        @pl.loop(1, DEPTH + 1)
        def _(t):
            qb = Q * mats[0, t - 1]
            s12, s13, s23 = cells[S12, t], cells[S13, t], cells[S23, t]
            s11, s22, s33 = cells[S11, t], cells[S22, t], cells[S33, t]
            cells[0, t] = cells[0, t] + qb * (
                cells[S11, t + 1] - s11 + (s12 - north(s12)) + (s13 - west(s13))
            )
            cells[1, t] = cells[1, t] + qb * (
                south(s22) - s22 + (s12 - cells[S12, t - 1]) + (s23 - west(s23))
            )
            cells[2, t] = cells[2, t] + qb * (
                east(s33) - s33 + (s13 - cells[S13, t - 1]) + (s23 - north(s23))
            )

        @pl.loop(1, DEPTH + 1)
        def _(t):
            la, m = Q * mats[1, t - 1], Q * mats[2, t - 1]
            v1, v2, v3 = cells[0, t], cells[1, t], cells[2, t]
            d1, d2, d3 = v1 - cells[0, t - 1], v2 - north(v2), v3 - west(v3)
            dil = la * (d1 + d2 + d3)
            m2 = 2.0 * m
            new = [
                cells[S11, t] + (dil + m2 * d1),
                cells[S22, t] + (dil + m2 * d2),
                cells[S33, t] + (dil + m2 * d3),
                cells[S23, t] + m * (east(v2) - v2 + (south(v3) - v3)),
                cells[S13, t] + m * (east(v1) - v1 + (cells[2, t + 1] - v3)),
                cells[S12, t] + m * (south(v1) - v1 + (cells[1, t + 1] - v2)),
            ]
            if step == 0:
                for f, x in enumerate(new):
                    cells[3 + f, t] = x
            else:
                for f, x in enumerate([v1, v2, v3] + new):
                    slab_out[f, t - 1] = x[0:R, 0:LANES]


def call(kernel, out_shape, flops, *args, scratch=()):
    many = isinstance(out_shape, (list, tuple))
    outs = list(out_shape) if many else [out_shape]
    n_bytes = sum(a.size * a.dtype.itemsize for a in args) + sum(math.prod(o.shape) * o.dtype.itemsize for o in outs)
    return pl.pallas_call(
        kernel,
        out_shape=out_shape,
        in_specs=[VMEM] * len(args),
        out_specs=[VMEM] * len(outs) if many else VMEM,
        scratch_shapes=scratch,
        compiler_params=pltpu.CompilerParams(vmem_limit_bytes=40 * 1024 * 1024),
        cost_estimate=pl.CostEstimate(flops=flops, bytes_accessed=n_bytes, transcendentals=0),
    )(*args)


def swap(x, axis, start):
    pairs = []
    for i in range(start, lax.axis_size(axis) - 1, 2):
        pairs += [(i, i + 1), (i + 1, i)]
    return lax.ppermute(x, axis, pairs)


def on_device(slab_state, buoyancy, lame_lambda, lame_mu, face_map, band_widths, ocean_state, water_depth):
    n_blk = lax.axis_size("blk")
    n_face = face_map.shape[0]
    arr = jax.ShapeDtypeStruct
    own = (slab_state, buoyancy, lame_lambda, lame_mu, ocean_state, water_depth)
    message = arr((SEC_TILES, 8, LANES), F32)
    first, second = call(pack_kernel, (message, message), 10**6, *own, band_widths)
    first = swap(first, "sec", 1)
    second = swap(second, "sec", 0)
    send, strips = call(
        uplift_kernel,
        (arr((n_blk, BLK_TILES, 8, LANES), F32), arr((96, 8, LANES), F32)),
        10**7,
        *own,
        first,
        second,
    )
    recv = lax.all_to_all(send, "blk", 0, 0, tiled=True)
    kernels = arr((3, COLS + 16, n_face), BF16)
    hi, lo = call(
        filter_kernel, (kernels, kernels), 10**8, face_map.reshape(1, n_face), band_widths, first, second
    )
    return call(
        final_kernel,
        (arr(slab_state.shape, F32), arr(ocean_state.shape, F32)),
        10**8,
        *own,
        first,
        second,
        strips,
        recv,
        hi,
        lo,
        scratch=[
            pltpu.VMEM((9, DEPTH + 2, 24, 2 * LANES), F32),
            pltpu.VMEM((3, DEPTH, 24, 2 * LANES), F32),
            pltpu.VMEM((5 * LANES, LANES), F32),
        ],
    )


def solution(mesh):
    in_specs = (
        P(None, None, "sec", "blk"),
        P(None, "sec", "blk"),
        P(None, "sec", "blk"),
        P(None, "sec", "blk"),
        P(),
        P("sec", None),
        P(None, "sec", "blk"),
        P("sec", "blk"),
    )
    out_specs = (P(None, None, "sec", "blk"), P(None, "sec", "blk"))
    return jax.shard_map(on_device, mesh=mesh, in_specs=in_specs, out_specs=out_specs, check_vma=False)
```

```python
import math

import jax
import jax.numpy as jnp
from jax import lax
from jax.experimental import pallas as pl
from jax.experimental.pallas import tpu as pltpu
from jax.sharding import PartitionSpec as P

Q = 0.25
R = 16
LANES = 128
DEPTH = 8
COLS = 512
S11, S22, S33, S23, S13, S12, BUO, LAM, MU = 3, 4, 5, 6, 7, 8, 9, 10, 11
UP_PLANES = [(S11, 0), (S11, 1), (S11, 2)] + [
    (f, t) for f in (S12, S13, S23, S22, S33, 0, 1, 2, BUO, LAM, MU) for t in (0, 1)
]
N_UP = len(UP_PLANES)
UP_INDEX = {ft: i for i, ft in enumerate(UP_PLANES)}
REST = [(f, t) for f in range(12) for t in range(DEPTH) if (f, t) not in UP_INDEX]
STRIP = N_UP
MISC = STRIP + (len(REST) + 3) // 4
OCEAN = MISC + 1
SEC_TILES = OCEAN + 16
B_UP, B_FACTOR, B_SLAB, B_OCEAN, BLK_TILES = 0, 4, 6, 11, 12
SPAN = 16
F32 = jnp.float32
BF16 = jnp.bfloat16
VMEM = pl.BlockSpec(memory_space=pltpu.VMEM)


def lane_iota(shape):
    return lax.broadcasted_iota(jnp.int32, shape, len(shape) - 1)


def row_iota(shape):
    return lax.broadcasted_iota(jnp.int32, shape, 0)


def reader(slab, mats):
    def read(f, t, rows):
        return slab[f, t, rows, :] if f < 9 else mats[f - 9][t, rows, :]

    return read


def pack_kernel(*refs):
    sources, widths, first, second = refs[:6], refs[6], refs[7], refs[8]
    copies, sem = refs[9:15], refs[15]
    moves = [pltpu.make_async_copy(a, c, sem.at[i]) for i, (a, c) in enumerate(zip(sources, copies))]
    for move in moves:
        move.start()
    for move in moves:
        move.wait()
    slab, buo, lam, mu, ocean, depth = copies
    odd = lax.rem(lax.axis_index("sec"), 2)
    read = reader(slab, (buo, lam, mu))
    for out, lower in ((first, odd), (second, 1 - odd)):
        start = pl.multiple_of(lower * 8, 8)
        rows = pl.ds(start, 8)
        for i, (f, t) in enumerate(UP_PLANES):
            out[i] = read(f, t, rows)
        out[MISC - 1] = jnp.zeros((8, LANES), F32)
        for p, (f, t) in enumerate(REST):
            strip = jnp.where(lower == 1, read(f, t, slice(14, 16)), read(f, t, slice(0, 2)))
            out[STRIP + p // 4, 2 * (p % 4) : 2 * (p % 4) + 2, :] = strip
        out[MISC] = jnp.zeros((8, LANES), F32)
        for t in (0, 1):
            out[MISC, t : t + 1, :] = read(S12, t, slice(7, 8))
        out[MISC, 2:3, 0 : widths.shape[1]] = widths[...].astype(F32)
        for f in range(4):
            for k in range(4):
                cols = slice(k * LANES, (k + 1) * LANES)
                out[OCEAN + 4 * f + k] = ocean[f, rows, cols] if f < 3 else depth[rows, cols]


def sides(first, second):
    odd = lax.rem(lax.axis_index("sec"), 2)

    def top(i):
        return jnp.where(odd == 0, first[i], second[i])

    def bottom(i):
        return jnp.where(odd == 0, second[i], first[i])

    return top, bottom


def uplift_kernel(slab, buo, lam, mu, ocean, depth, first, second, send, strips, windows):
    me = lax.axis_index("blk")
    read = reader(slab, (buo, lam, mu))
    top, bottom = sides(first, second)
    shape = (32, LANES)
    lane, row = lane_iota(shape), row_iota(shape)

    def plane(f, t):
        i = UP_INDEX[(f, t)]
        return jnp.concatenate([top(i), read(f, t, slice(0, 16)), bottom(i)], axis=0)

    def north(x):
        return pltpu.roll(x, 1, 0)

    def south(x):
        return pltpu.roll(x, 31, 0)

    def west(x):
        return jnp.where(lane == 0, 0.0, pltpu.roll(x, 1, 1))

    def east(x):
        return jnp.where(lane == LANES - 1, 0.0, pltpu.roll(x, LANES - 1, 1))

    s11 = [plane(S11, t) for t in range(3)]
    s22, s33, s23, s13, s12 = ([plane(f, t) for t in (0, 1)] for f in (S22, S33, S23, S13, S12))
    b, la, m = ([plane(f, t) for t in (0, 1)] for f in (BUO, LAM, MU))
    misc = top(MISC)
    v1, v2, v3 = [], [], []
    for t in (0, 1):
        above = lambda s: s[t] - s[t - 1] if t else s[t]
        s12n = jnp.where(row == 0, misc[t : t + 1, :], north(s12[t]))
        v1.append(plane(0, t) + Q * b[t] * (s11[t + 1] - s11[t] + (s12[t] - s12n) + (s13[t] - west(s13[t]))))
        v2.append(plane(1, t) + Q * b[t] * (south(s22[t]) - s22[t] + above(s12) + (s23[t] - west(s23[t]))))
        v3.append(plane(2, t) + Q * b[t] * (east(s33[t]) - s33[t] + above(s13) + (s23[t] - north(s23[t]))))
    n11 = []
    for t in (0, 1):
        d1 = v1[t] - v1[t - 1] if t else v1[t]
        dil = d1 + (v2[t] - north(v2[t])) + (v3[t] - west(v3[t]))
        n11.append(s11[t] + Q * (la[t] * dil + 2.0 * m[t] * d1))
    n12 = s12[0] + Q * m[0] * (south(v1[0]) - v1[0] + v2[1] - v2[0])
    n13 = s13[0] + Q * m[0] * (east(v1[0]) - v1[0] + v3[1] - v3[0])
    g = Q * Q * b[0]
    rise = 2.0 * Q * v1[0] + g * (n11[1] - n11[0] + n12 - north(n12) + n13 - west(n13))

    la0, la1 = Q * la[0], Q * la[1]
    m0, m1 = la0 + 2.0 * Q * m[0], la1 + 2.0 * Q * m[1]
    q0 = Q * m[0]
    q0n = north(q0)
    b0, b1 = Q * b[0], Q * b[1]
    left = [
        g * (la1 + q0) * b1,
        -g * (la0 + q0) * b0,
        g * q0,
        g * q0 * s13[0],
        s13[0],
        south(s13[0]),
        north(s13[0]),
        s13[1],
        s23[0],
        north(s23[0]),
        s23[1],
        north(s23[1]),
        v3[1],
        b1,
        v3[0],
        b0,
        n13,
        q0,
        q0 * s13[0],
        q0 * b1,
        q0 * b0,
        s13[0],
    ]
    right = [
        s33[1],
        s33[0],
        v1[0],
        -b0,
        -(2.0 * Q - g * (m1 + m0 + 2.0 * q0 + q0n)) * b0,
        -g * q0 * south(b0),
        -g * q0n * north(b0),
        -g * m1 * b1,
        g * (la0 + q0) * b0,
        -g * (la0 + q0n) * north(b0),
        -g * (la1 + q0) * b1,
        g * (la1 + q0n) * north(b1),
        -g * la1,
        -g * la1 * s33[1],
        g * la0,
        g * la0 * s33[0],
        -g,
        -g * v1[0],
        g * b0,
        -g * s33[1],
        g * s33[0],
        -pltpu.roll(g, LANES - 1, 1) * q0 * b0,
    ]
    factors = jnp.zeros(shape, F32)
    for i, (x, y) in enumerate(zip(left, right)):
        factors = jnp.where(lane == i, pltpu.roll(x, (i + 1) % LANES, 1), factors)
        factors = jnp.where(lane == 32 + i, pltpu.roll(y, 32 + i, 1), factors)
    packed = jnp.where(lane[:16] < 64, factors[:16], pltpu.roll(factors[16:], 64, 1))

    tile = (8, LANES)
    tlane, trow = lane_iota(tile), row_iota(tile)
    odd = lax.rem(lax.axis_index("sec"), 2)
    for i, (f, t) in enumerate(UP_PLANES):
        strips[f, t] = jnp.where(trow < 2, bottom(i), jnp.where(trow >= 6, top(i), 0.0))
    for p, (f, t) in enumerate(REST):
        i, at = STRIP + p // 4, slice(2 * (p % 4), 2 * (p % 4) + 2)
        a, c = first[i, at, :], second[i, at, :]
        strips[f, t] = jnp.zeros(tile, F32)
        strips[f, t, 0:2, :] = jnp.where(odd == 0, c, a)
        strips[f, t, 6:8, :] = jnp.where(odd == 0, a, c)
    heads = [jnp.zeros(tile, F32) for _ in range(5)]
    tails = [jnp.zeros(tile, F32) for _ in range(5)]
    spot = tlane % SPAN
    for f in range(12):
        for r in range(3):
            near, far = jnp.zeros(tile, F32), jnp.zeros(tile, F32)
            for t in range(DEPTH):
                at = SPAN * t
                x = read(f, t, slice(8 * r, 8 * r + 8)) if r < 2 else strips[f, t]
                x = pltpu.roll(x, (at + 8) % LANES, 1)
                near = jnp.where((tlane >= at + 8) & (tlane < at + 12), x, near)
                far = jnp.where((tlane >= at + 4) & (tlane < at + 8), x, far)
            windows[0, f, 8 * r : 8 * r + 8, :] = near
            windows[1, f, 8 * r : 8 * r + 8, :] = far
            i = f * 3 + r
            k, at = i // 8, 2 * (i % 8)
            here = (spot >= at) & (spot < at + 2)
            heads[k] = jnp.where(here, pltpu.roll(near, (at - 8) % LANES, 1), heads[k])
            tails[k] = jnp.where(here, pltpu.roll(far, (at - 6) % LANES, 1), tails[k])
    head, tail = jnp.zeros(tile, F32), jnp.zeros(tile, F32)
    for f in range(4):
        for r in range(4):
            at = 32 * f + 8 * r
            ends = []
            for k in (0, 3):
                cols = slice(k * LANES, (k + 1) * LANES)
                rows = slice(8 * r - 8, 8 * r)
                if r == 0:
                    x = top(OCEAN + 4 * f + k)
                elif r == 3:
                    x = bottom(OCEAN + 4 * f + k)
                else:
                    x = ocean[f, rows, cols] if f < 3 else depth[rows, cols]
                ends.append(x)
            here = (tlane >= at) & (tlane < at + 8)
            head = jnp.where(here, pltpu.roll(ends[0], at, 1), head)
            tail = jnp.where(here, pltpu.roll(ends[1], (at + 8) % LANES, 1), tail)
    heads.append(head)
    tails.append(tail)
    for d in range(send.shape[0]):
        for r in range(4):
            send[d, B_UP + r] = rise[8 * r : 8 * r + 8]
        for r in range(2):
            send[d, B_FACTOR + r] = packed[8 * r : 8 * r + 8]
        for i in range(6):
            send[d, B_SLAB + i] = jnp.where(d < me, heads[i], tails[i])


def middle_kernel(
    slab, buo, lam, mu, ocean, depth, first, second, strips, face, widths, plain, seas, filters, cells, mats
):
    me = lax.axis_index("blk")
    top, bottom = sides(first, second)
    read = reader(slab, (buo, lam, mu))
    lane = lane_iota((1, LANES))
    face_at = (face[...] - me * COLS).astype(F32)
    width = face.shape[1]

    def scales(row):
        out = []
        for j in (me, me + 1, me - 1):
            w = jnp.sum(jnp.where(lane[:, : row.shape[1]] == j, row, 0.0), axis=1, keepdims=True)
            w = jnp.where(w > 0.0, w, 1.0)
            out.append((-(math.pi / 2.0) * math.log2(math.e) / w, 1.0 / w))
        return out

    groups = [scales(top(MISC)[2:3, :]), scales(widths[...].astype(F32)), scales(bottom(MISC)[2:3, :])]

    def put(k, rows, distance, rate, gain):
        decay = jnp.exp2(distance * rate)
        value = decay / (1.0 + decay * decay) * gain
        upper = value.astype(BF16)
        filters[rows, k * width : (k + 1) * width] = upper
        filters[rows, (3 + k) * width : (4 + k) * width] = (value - upper.astype(F32)).astype(BF16)

    @pl.loop(0, COLS // 16)
    def _(c):
        start = pl.multiple_of(c * 16, 16)
        at = (lax.broadcasted_iota(jnp.int32, (16, width), 0) + start).astype(F32)
        distance = jnp.abs(at - face_at)
        for k in range(3):
            put(k, pl.ds(start, 16), distance, *groups[k][0])

    row = row_iota((16, width))
    at = jnp.where(row < 8, row + COLS, row - 16).astype(F32)
    distance = jnp.abs(at - face_at)
    for k in range(3):
        rate = jnp.where(row < 8, groups[k][1][0], groups[k][2][0])
        gain = jnp.where(row < 8, groups[k][1][1], groups[k][2][1])
        put(k, slice(COLS, COLS + 16), distance, rate, gain)

    for f in range(4):
        for k in range(4):
            cols = slice(k * LANES, (k + 1) * LANES)
            i = OCEAN + 4 * f + k
            seas[f, 0:8, cols] = top(i)
            seas[f, 8:24, cols] = ocean[f, :, cols] if f < 3 else depth[:, cols]
            seas[f, 24:32, cols] = bottom(i)

    for f in range(9):
        for t in (0, DEPTH + 1):
            cells[f, t] = jnp.zeros((24, LANES), F32)
    for f in range(12):
        for t in range(DEPTH):
            if f < 9:
                cells[f, t + 1, 0:R, :] = slab[f, t]
                cells[f, t + 1, R:, :] = strips[f, t]
            else:
                mats[f - 9, t, 0:R, :] = (buo, lam, mu)[f - 9][t]
                mats[f - 9, t, R:, :] = strips[f, t]
    north = lambda v: pltpu.roll(v, 1, 0)
    south = lambda v: pltpu.roll(v, 23, 0)
    west = lambda v: pltpu.roll(v, 1, 1)
    east = lambda v: pltpu.roll(v, LANES - 1, 1)
    for step in range(2):

        @pl.loop(1, DEPTH + 1)
        def _(t):
            s = [cells[3 + f, t] for f in range(6)]
            below, above = cells[S11, t + 1], (cells[S12, t - 1], cells[S13, t - 1])
            new = velocities([cells[a, t] for a in range(3)], s, Q * mats[0, t - 1], below, above, north, south, west, east)
            for a in range(3):
                cells[a, t] = new[a]

        @pl.loop(1, DEPTH + 1)
        def _(t):
            v = [cells[a, t] for a in range(3)]
            s = [cells[3 + f, t] for f in range(6)]
            below, above = (cells[1, t + 1], cells[2, t + 1]), cells[0, t - 1]
            new = stresses(s, v, Q * mats[1, t - 1], Q * mats[2, t - 1], below, above, north, south, west, east)
            if step == 0:
                for f in range(6):
                    cells[3 + f, t] = new[f]
            else:
                for f, x in enumerate(v + new):
                    plain[f, t - 1] = x[0:R]


def velocities(v, s, qb, s11_below, above, north, south, west, east):
    s11, s22, s33, s23, s13, s12 = s
    return [
        v[0] + qb * (s11_below - s11 + (s12 - north(s12)) + (s13 - west(s13))),
        v[1] + qb * (south(s22) - s22 + (s12 - above[0]) + (s23 - west(s23))),
        v[2] + qb * (east(s33) - s33 + (s13 - above[1]) + (s23 - north(s23))),
    ]


def stresses(s, v, la, m, below, v1_above, north, south, west, east):
    v1, v2, v3 = v
    d1, d2, d3 = v1 - v1_above, v2 - north(v2), v3 - west(v3)
    dil = la * (d1 + d2 + d3)
    m2 = 2.0 * m
    return [
        s[0] + (dil + m2 * d1),
        s[1] + (dil + m2 * d2),
        s[2] + (dil + m2 * d3),
        s[3] + m * (east(v2) - v2 + (south(v3) - v3)),
        s[4] + m * (east(v1) - v1 + (below[1] - v3)),
        s[5] + m * (south(v1) - v1 + (below[0] - v2)),
    ]


def final_kernel(plain, seas, filters, windows, recv, slab_out, ocean_out, flat):
    sec, me = lax.axis_index("sec"), lax.axis_index("blk")
    n_sec, n_blk = lax.axis_size("sec"), lax.axis_size("blk")
    shape = (32, LANES)
    lane, row = lane_iota(shape), row_iota(shape)
    before, after = jnp.maximum(me - 1, 0), jnp.minimum(me + 1, n_blk - 1)
    west_on, east_on = me > 0, me < n_blk - 1
    tile = (8, LANES)
    tlane = lane_iota(tile)

    rises = [jnp.concatenate([recv[j, B_UP + r] for r in range(4)], axis=0) for j in range(n_blk)]
    factors = []
    for j in range(n_blk):
        x = jnp.concatenate([recv[j, B_FACTOR], recv[j, B_FACTOR + 1]], axis=0)
        factors.append(jnp.concatenate([x, pltpu.roll(x, 64, 1)], axis=0))
    for j in range(n_blk - 1):
        terms = factors[j] * pltpu.roll(factors[j + 1], LANES - 32, 1)
        pick = lambda a, z: jnp.sum(jnp.where((lane >= a) & (lane < z), terms, 0.0), axis=1, keepdims=True)
        rises[j] = rises[j] + jnp.where(lane == LANES - 1, pick(0, 4), 0.0)
        rises[j + 1] = rises[j + 1] + jnp.where(lane == 0, pick(4, 21), 0.0) + jnp.where(lane == 1, pick(21, 22), 0.0)
    rise = jnp.concatenate(rises, axis=1)
    rise_hi = rise.astype(BF16).astype(F32)
    rise_lo = rise - rise_hi
    wide = row_iota(rise.shape)
    upper, lower = [], []
    for k in range(3):
        mine = (wide >= (0, 8, 24)[k]) & (wide < (8, 24, 32)[k])
        part = jnp.where(mine, rise_hi, 0.0)
        upper.append(jnp.concatenate([part, jnp.where(mine, rise_lo, 0.0)], axis=0))
        lower.append(jnp.concatenate([part, jnp.zeros_like(part)], axis=0))
    both = jnp.concatenate(upper + lower, axis=1).astype(BF16)
    source = lax.dot_general(filters[...], both, (((1,), (1,)), ((), ())), preferred_element_type=F32)
    flat[...] = jnp.zeros((5 * LANES, LANES), F32)
    flat[0 : COLS + 8, 0:64] = source[0 : COLS + 8]
    flat[5 * LANES - 8 : 5 * LANES, 0:64] = source[COLS + 8 : COLS + 16]
    turned = [flat[k * LANES : (k + 1) * LANES, :].T for k in range(5)]
    source = jnp.concatenate([x[0:32] + x[32:64] for x in turned], axis=1)

    ring = (32, 5 * LANES)
    fields = []
    for f in range(4):
        halo = []
        for r in range(4):
            at = 32 * f + 8 * r
            east_in = pltpu.roll(recv[after, B_OCEAN], (LANES - at) % LANES, 1)
            west_in = pltpu.roll(recv[before, B_OCEAN], (2 * LANES - 8 - at) % LANES, 1)
            x = jnp.where((tlane < 8) & east_on, east_in, 0.0)
            halo.append(jnp.where((tlane >= LANES - 8) & west_on, west_in, x))
        fields.append(jnp.concatenate([seas[f], jnp.concatenate(halo, axis=0)], axis=1))
    surface, strike, dip, water = fields
    at = lane_iota(ring)
    at = jnp.where(at >= 5 * LANES - 8, at - 5 * LANES, at)
    x, y = row_iota(ring) - 8 + sec * R, at + me * COLS
    wet = (x >= 0) & (x < n_sec * R) & (y >= 0) & (y < n_blk * COLS) & (at < COLS + 8)
    surface = surface + source
    water = 0.25 * water
    for step in range(4):
        change = pltpu.roll(strike, 31, 0) - pltpu.roll(strike, 1, 0)
        change = change + (pltpu.roll(dip, 5 * LANES - 1, 1) - pltpu.roll(dip, 1, 1))
        surface = jnp.where(wet, surface - 0.25 * change, 0.0)
        strike = strike - water * (pltpu.roll(surface, 31, 0) - pltpu.roll(surface, 1, 0))
        dip = dip - water * (pltpu.roll(surface, 5 * LANES - 1, 1) - pltpu.roll(surface, 1, 1))
    ocean_out[0] = surface[8:24, 0:COLS]
    ocean_out[1] = strike[8:24, 0:COLS]
    ocean_out[2] = dip[8:24, 0:COLS]

    spot = tlane % SPAN
    north = lambda v: pltpu.roll(v, 1, 0)
    south = lambda v: pltpu.roll(v, 23, 0)
    west = lambda v: pltpu.roll(v, 1, 1)
    east = lambda v: pltpu.roll(v, LANES - 1, 1)
    wlane = lane_iota((24, LANES))
    above = lambda v: jnp.where(wlane < SPAN, 0.0, pltpu.roll(v, SPAN, 1))
    below = lambda v: jnp.where(wlane >= LANES - SPAN, 0.0, pltpu.roll(v, LANES - SPAN, 1))
    results = []
    for side in range(2):
        other, on, home = ((before, west_on, 6), (after, east_on, 8))[side]
        here = (spot >= home) & (spot < home + 2)
        state = []
        for f in range(12):
            parts = []
            for r in range(3):
                i = f * 3 + r
                x = pltpu.roll(recv[other, B_SLAB + i // 8], (home - 2 * (i % 8)) % LANES, 1)
                own = windows[side, f, 8 * r : 8 * r + 8, :]
                parts.append(jnp.where(here & on, x, own))
            state.append(jnp.concatenate(parts, axis=0))
        v, s = state[0:3], state[3:9]
        qb, la, m = Q * state[BUO], Q * state[LAM], Q * state[MU]
        for step in range(2):
            v = velocities(v, s, qb, below(s[0]), (above(s[5]), above(s[4])), north, south, west, east)
            s = stresses(s, v, la, m, (below(v[1]), below(v[2])), above(v[0]), north, south, west, east)
        results.append(v + s)
    edge = (tlane < 2) | (tlane >= LANES - 2)
    for f in range(9):
        for r in range(2):
            rows = slice(8 * r, 8 * r + 8)
            both = jnp.where(spot >= 8, results[0][f][rows], results[1][f][rows])
            for t in range(DEPTH):
                moved = pltpu.roll(both, (2 * LANES - SPAN * t - 8) % LANES, 1)
                slab_out[f, t, rows, :] = jnp.where(edge, moved, plain[f, t, rows, :])


def call(kernel, out_shape, flops, *args, far=0, scratch=()):
    many = isinstance(out_shape, (list, tuple))
    outs = list(out_shape) if many else [out_shape]
    n_bytes = sum(a.size * a.dtype.itemsize for a in args) + sum(math.prod(o.shape) * o.dtype.itemsize for o in outs)
    return pl.pallas_call(
        kernel,
        out_shape=out_shape,
        in_specs=[pl.BlockSpec(memory_space=pltpu.HBM)] * far + [VMEM] * (len(args) - far),
        out_specs=[VMEM] * len(outs) if many else VMEM,
        scratch_shapes=scratch,
        compiler_params=pltpu.CompilerParams(vmem_limit_bytes=12 * 1024 * 1024),
        cost_estimate=pl.CostEstimate(flops=flops, bytes_accessed=n_bytes, transcendentals=0),
    )(*args)


def swap(x, axis, start):
    pairs = []
    for i in range(start, lax.axis_size(axis) - 1, 2):
        pairs += [(i, i + 1), (i + 1, i)]
    return lax.ppermute(x, axis, pairs)


def on_device(slab_state, buoyancy, lame_lambda, lame_mu, face_map, band_widths, ocean_state, water_depth):
    n_blk = lax.axis_size("blk")
    n_face = face_map.shape[0]
    arr = jax.ShapeDtypeStruct
    own = (slab_state, buoyancy, lame_lambda, lame_mu, ocean_state, water_depth)
    message = arr((SEC_TILES, 8, LANES), F32)
    first, second = call(
        pack_kernel,
        (message, message),
        10**6,
        *own,
        band_widths,
        far=6,
        scratch=[pltpu.VMEM(a.shape, F32) for a in own] + [pltpu.SemaphoreType.DMA((6,))],
    )
    first = swap(first, "sec", 1)
    second = swap(second, "sec", 0)
    send, strips, windows = call(
        uplift_kernel,
        (
            arr((n_blk, BLK_TILES, 8, LANES), F32),
            arr((12, DEPTH, 8, LANES), F32),
            arr((2, 12, 24, LANES), F32),
        ),
        10**7,
        *own,
        first,
        second,
    )
    recv = lax.all_to_all(send, "blk", 0, 0, tiled=True)
    plain, seas, filters = call(
        middle_kernel,
        (
            arr(slab_state.shape, F32),
            arr((4, 32, COLS), F32),
            arr((COLS + 16, 6 * n_face), BF16),
        ),
        10**8,
        *own,
        first,
        second,
        strips,
        face_map.reshape(1, n_face),
        band_widths,
        scratch=[
            pltpu.VMEM((9, DEPTH + 2, 24, LANES), F32),
            pltpu.VMEM((3, DEPTH, 24, LANES), F32),
        ],
    )
    return call(
        final_kernel,
        (arr(slab_state.shape, F32), arr(ocean_state.shape, F32)),
        10**8,
        plain,
        seas,
        filters,
        windows,
        recv,
        scratch=[pltpu.VMEM((5 * LANES, LANES), F32)],
    )


def solution(mesh):
    in_specs = (
        P(None, None, "sec", "blk"),
        P(None, "sec", "blk"),
        P(None, "sec", "blk"),
        P(None, "sec", "blk"),
        P(),
        P("sec", None),
        P(None, "sec", "blk"),
        P("sec", "blk"),
    )
    out_specs = (P(None, None, "sec", "blk"), P(None, "sec", "blk"))
    return jax.shard_map(on_device, mesh=mesh, in_specs=in_specs, out_specs=out_specs, check_vma=False)
```

```python
import math

import jax
import jax.numpy as jnp
from jax import lax
from jax.experimental import pallas as pl
from jax.experimental.pallas import tpu as pltpu
from jax.sharding import PartitionSpec as P

Q = 0.25
R = 16
LANES = 128
DEPTH = 8
COLS = 512
S11, S22, S33, S23, S13, S12, BUO, LAM, MU = 3, 4, 5, 6, 7, 8, 9, 10, 11
UP_PLANES = [(S11, 0), (S11, 1), (S11, 2)] + [
    (f, t) for f in (S12, S13, S23, S22, S33, 0, 1, 2, BUO, LAM, MU) for t in (0, 1)
]
N_UP = len(UP_PLANES)
UP_INDEX = {ft: i for i, ft in enumerate(UP_PLANES)}
REST = [(f, t) for f in range(12) for t in range(DEPTH) if (f, t) not in UP_INDEX]
STRIP = N_UP
MISC = STRIP + (len(REST) + 3) // 4
OCEAN = MISC + 1
SEC_TILES = OCEAN + 16
B_UP, B_FACTOR, B_SLAB, B_OCEAN, BLK_TILES = 0, 4, 6, 11, 12
SPAN = 16
F32 = jnp.float32
MIB = 1 << 20
BF16 = jnp.bfloat16
VMEM = pl.BlockSpec(memory_space=pltpu.VMEM)


def lane_iota(shape):
    return lax.broadcasted_iota(jnp.int32, shape, len(shape) - 1)


def row_iota(shape):
    return lax.broadcasted_iota(jnp.int32, shape, 0)


def fetch(sources, targets, sem):
    moves = [pltpu.make_async_copy(a, b, sem.at[i]) for i, (a, b) in enumerate(zip(sources, targets))]
    for move in moves:
        move.start()
    for move in moves:
        move.wait()


def pack_kernel(*refs):
    sources, (first, second), copies, sem = refs[:7], refs[7:9], refs[9:16], refs[16]
    fetch(sources, copies, sem)
    widths = copies[6]
    slab, buo, lam, mu, ocean, depth = copies[:6]
    odd = lax.rem(lax.axis_index("sec"), 2)

    def read(f, t, rows):
        return slab[f, t, rows, :] if f < 9 else (buo, lam, mu)[f - 9][t, rows, :]

    for out, lower in ((first, odd), (second, 1 - odd)):
        start = pl.multiple_of(lower * 8, 8)
        rows = pl.ds(start, 8)
        for i, (f, t) in enumerate(UP_PLANES):
            out[i] = read(f, t, rows)
        out[MISC - 1] = jnp.zeros((8, LANES), F32)
        for p, (f, t) in enumerate(REST):
            strip = jnp.where(lower == 1, read(f, t, slice(14, 16)), read(f, t, slice(0, 2)))
            out[STRIP + p // 4, 2 * (p % 4) : 2 * (p % 4) + 2, :] = strip
        out[MISC] = jnp.zeros((8, LANES), F32)
        for t in (0, 1):
            out[MISC, t : t + 1, :] = read(S12, t, slice(7, 8))
        out[MISC, 2:3, 0 : widths.shape[1]] = widths[...].astype(F32)
        for f in range(4):
            for k in range(4):
                cols = slice(k * LANES, (k + 1) * LANES)
                out[OCEAN + 4 * f + k] = ocean[f, rows, cols] if f < 3 else depth[rows, cols]


def sides(first, second):
    odd = lax.rem(lax.axis_index("sec"), 2)

    def top(i):
        return jnp.where(odd == 0, first[i], second[i])

    def bottom(i):
        return jnp.where(odd == 0, second[i], first[i])

    return top, bottom


def edges(x, r, tlane):
    out = None
    for t in range(DEPTH):
        moved = pltpu.roll(x[t, 8 * r : 8 * r + 8], (SPAN * t + 8) % LANES, 1)
        out = moved if t == 0 else jnp.where(tlane >= SPAN * t, moved, out)
    return out


def halo_spot(f, r, tlane):
    i = f * 3 + r
    at = 2 * (i % 8)
    spot = tlane % SPAN
    return i // 8, at, (spot >= at) & (spot < at + 2)


def carry_kernel(slab, buo, lam, mu, ocean, depth, state, sea, windows, halos):
    state[0:9] = slab[...]
    for i, x in enumerate((buo, lam, mu)):
        state[9 + i] = x[...]
    sea[0:3] = ocean[...]
    sea[3] = depth[...]
    tlane = lane_iota((8, LANES))
    heads = [jnp.zeros((8, LANES), F32) for _ in range(5)]
    tails = [jnp.zeros((8, LANES), F32) for _ in range(5)]
    for f in range(12):
        for r in range(2):
            x = edges(slab.at[f] if f < 9 else (buo, lam, mu)[f - 9], r, tlane)
            windows[f, 8 * r : 8 * r + 8, :] = x
            k, at, here = halo_spot(f, r, tlane)
            heads[k] = jnp.where(here, pltpu.roll(x, (at - 8) % LANES, 1), heads[k])
            tails[k] = jnp.where(here, pltpu.roll(x, (at - 6) % LANES, 1), tails[k])
    for k in range(5):
        halos[0, k] = heads[k]
        halos[1, k] = tails[k]


def uplift_kernel(state, sea, halos, first, second, send, strips, last):
    me = lax.axis_index("blk")
    top, bottom = sides(first, second)
    shape = (32, LANES)
    lane, row = lane_iota(shape), row_iota(shape)

    def plane(f, t):
        i = UP_INDEX[(f, t)]
        return jnp.concatenate([top(i), state[f, t], bottom(i)], axis=0)

    def north(x):
        return pltpu.roll(x, 1, 0)

    def south(x):
        return pltpu.roll(x, 31, 0)

    def west(x):
        return jnp.where(lane == 0, 0.0, pltpu.roll(x, 1, 1))

    def east(x):
        return jnp.where(lane == LANES - 1, 0.0, pltpu.roll(x, LANES - 1, 1))

    s11 = [plane(S11, t) for t in range(3)]
    s22, s33, s23, s13, s12 = ([plane(f, t) for t in (0, 1)] for f in (S22, S33, S23, S13, S12))
    b, la, m = ([plane(f, t) for t in (0, 1)] for f in (BUO, LAM, MU))
    misc = top(MISC)
    v1, v2, v3 = [], [], []
    for t in (0, 1):
        above = lambda s: s[t] - s[t - 1] if t else s[t]
        s12n = jnp.where(row == 0, misc[t : t + 1, :], north(s12[t]))
        v1.append(plane(0, t) + Q * b[t] * (s11[t + 1] - s11[t] + (s12[t] - s12n) + (s13[t] - west(s13[t]))))
        v2.append(plane(1, t) + Q * b[t] * (south(s22[t]) - s22[t] + above(s12) + (s23[t] - west(s23[t]))))
        v3.append(plane(2, t) + Q * b[t] * (east(s33[t]) - s33[t] + above(s13) + (s23[t] - north(s23[t]))))
    n11 = []
    for t in (0, 1):
        d1 = v1[t] - v1[t - 1] if t else v1[t]
        dil = d1 + (v2[t] - north(v2[t])) + (v3[t] - west(v3[t]))
        n11.append(s11[t] + Q * (la[t] * dil + 2.0 * m[t] * d1))
    n12 = s12[0] + Q * m[0] * (south(v1[0]) - v1[0] + v2[1] - v2[0])
    n13 = s13[0] + Q * m[0] * (east(v1[0]) - v1[0] + v3[1] - v3[0])
    g = Q * Q * b[0]
    rise = 2.0 * Q * v1[0] + g * (n11[1] - n11[0] + n12 - north(n12) + n13 - west(n13))

    la0, la1 = Q * la[0], Q * la[1]
    m0, m1 = la0 + 2.0 * Q * m[0], la1 + 2.0 * Q * m[1]
    q0 = Q * m[0]
    q0n = north(q0)
    b0, b1 = Q * b[0], Q * b[1]
    left = [
        g * (la1 + q0) * b1,
        -g * (la0 + q0) * b0,
        g * q0,
        g * q0 * s13[0],
        s13[0],
        south(s13[0]),
        north(s13[0]),
        s13[1],
        s23[0],
        north(s23[0]),
        s23[1],
        north(s23[1]),
        v3[1],
        b1,
        v3[0],
        b0,
        n13,
        q0,
        q0 * s13[0],
        q0 * b1,
        q0 * b0,
        s13[0],
    ]
    right = [
        s33[1],
        s33[0],
        v1[0],
        -b0,
        -(2.0 * Q - g * (m1 + m0 + 2.0 * q0 + q0n)) * b0,
        -g * q0 * south(b0),
        -g * q0n * north(b0),
        -g * m1 * b1,
        g * (la0 + q0) * b0,
        -g * (la0 + q0n) * north(b0),
        -g * (la1 + q0) * b1,
        g * (la1 + q0n) * north(b1),
        -g * la1,
        -g * la1 * s33[1],
        g * la0,
        g * la0 * s33[0],
        -g,
        -g * v1[0],
        g * b0,
        -g * s33[1],
        g * s33[0],
        -pltpu.roll(g, LANES - 1, 1) * q0 * b0,
    ]
    factors = jnp.zeros(shape, F32)
    for i, (x, y) in enumerate(zip(left, right)):
        factors = jnp.where(lane == i, pltpu.roll(x, (i + 1) % LANES, 1), factors)
        factors = jnp.where(lane == 32 + i, pltpu.roll(y, 32 + i, 1), factors)
    packed = jnp.where(lane[:16] < 64, factors[:16], pltpu.roll(factors[16:], 64, 1))

    tile = (8, LANES)
    tlane, trow = lane_iota(tile), row_iota(tile)
    odd = lax.rem(lax.axis_index("sec"), 2)
    for i, (f, t) in enumerate(UP_PLANES):
        strips[f, t] = jnp.where(trow < 2, bottom(i), jnp.where(trow >= 6, top(i), 0.0))
    for p, (f, t) in enumerate(REST):
        i, at = STRIP + p // 4, slice(2 * (p % 4), 2 * (p % 4) + 2)
        a, c = first[i, at, :], second[i, at, :]
        strips[f, t] = jnp.zeros(tile, F32)
        strips[f, t, 0:2, :] = jnp.where(odd == 0, c, a)
        strips[f, t, 6:8, :] = jnp.where(odd == 0, a, c)
    heads = [halos[0, k] for k in range(5)]
    tails = [halos[1, k] for k in range(5)]
    for f in range(12):
        x = edges(strips.at[f], 0, tlane)
        last[f] = x
        k, at, here = halo_spot(f, 2, tlane)
        heads[k] = jnp.where(here, pltpu.roll(x, (at - 8) % LANES, 1), heads[k])
        tails[k] = jnp.where(here, pltpu.roll(x, (at - 6) % LANES, 1), tails[k])
    head, tail = jnp.zeros(tile, F32), jnp.zeros(tile, F32)
    for f in range(4):
        for r in range(4):
            at = 32 * f + 8 * r
            ends = []
            for k in (0, 3):
                cols = slice(k * LANES, (k + 1) * LANES)
                rows = slice(8 * r - 8, 8 * r)
                if r == 0:
                    x = top(OCEAN + 4 * f + k)
                elif r == 3:
                    x = bottom(OCEAN + 4 * f + k)
                else:
                    x = sea[f, rows, cols]
                ends.append(x)
            here = (tlane >= at) & (tlane < at + 8)
            head = jnp.where(here, pltpu.roll(ends[0], at, 1), head)
            tail = jnp.where(here, pltpu.roll(ends[1], (at + 8) % LANES, 1), tail)
    heads.append(head)
    tails.append(tail)
    for d in range(send.shape[0]):
        for r in range(4):
            send[d, B_UP + r] = rise[8 * r : 8 * r + 8]
        for r in range(2):
            send[d, B_FACTOR + r] = packed[8 * r : 8 * r + 8]
        for i in range(6):
            send[d, B_SLAB + i] = jnp.where(d < me, heads[i], tails[i])


def filter_moves(source, target, sem):
    rows = [slice(k * LANES, (k + 1) * LANES + (16 if k == 3 else 0)) for k in range(4)]
    return [pltpu.make_async_copy(source.at[at, :], target.at[at, :], sem.at[k]) for k, at in enumerate(rows)]


def middle_kernel(state, sea, first, second, strips, face, widths, plain, seas, filters, cells, mats, held, sem):
    me = lax.axis_index("blk")
    top, bottom = sides(first, second)
    lane = lane_iota((1, LANES))
    face_at = (face[...] - me * COLS).astype(F32)
    width = face.shape[1]

    def scales(row):
        out = []
        for j in (me, me + 1, me - 1):
            w = jnp.sum(jnp.where(lane[:, : row.shape[1]] == j, row, 0.0), axis=1, keepdims=True)
            w = jnp.where(w > 0.0, w, 1.0)
            out.append((-(math.pi / 2.0) * math.log2(math.e) / w, 1.0 / w))
        return out

    groups = [scales(top(MISC)[2:3, :]), scales(widths[...].astype(F32)), scales(bottom(MISC)[2:3, :])]

    def put(k, rows, distance, rate, gain):
        decay = jnp.exp2(distance * rate)
        value = decay / (1.0 + decay * decay) * gain
        upper = value.astype(BF16)
        held[rows, k * width : (k + 1) * width] = upper
        held[rows, (3 + k) * width : (4 + k) * width] = (value - upper.astype(F32)).astype(BF16)

    row = row_iota((16, width))
    at = jnp.where(row < 8, row + COLS, row - 16).astype(F32)
    distance = jnp.abs(at - face_at)
    for k in range(3):
        rate = jnp.where(row < 8, groups[k][1][0], groups[k][2][0])
        gain = jnp.where(row < 8, groups[k][1][1], groups[k][2][1])
        put(k, slice(COLS, COLS + 16), distance, rate, gain)
    moves = filter_moves(held, filters, sem)
    for piece in range(4):

        @pl.loop(piece * LANES // 16, (piece + 1) * LANES // 16)
        def _(c):
            start = pl.multiple_of(c * 16, 16)
            at = (lax.broadcasted_iota(jnp.int32, (16, width), 0) + start).astype(F32)
            distance = jnp.abs(at - face_at)
            for k in range(3):
                put(k, pl.ds(start, 16), distance, *groups[k][0])

        moves[piece].start()

    for f in range(4):
        for k in range(4):
            cols = slice(k * LANES, (k + 1) * LANES)
            i = OCEAN + 4 * f + k
            seas[f, 0:8, cols] = top(i)
            seas[f, 8:24, cols] = sea[f, :, cols]
            seas[f, 24:32, cols] = bottom(i)

    for f in range(9):
        for t in (0, DEPTH + 1):
            cells[f, t] = jnp.zeros((24, LANES), F32)
    for f in range(12):
        for t in range(DEPTH):
            if f < 9:
                cells[f, t + 1, 0:R, :] = state[f, t]
                cells[f, t + 1, R:, :] = strips[f, t]
            else:
                mats[f - 9, t, 0:R, :] = state[f, t]
                mats[f - 9, t, R:, :] = strips[f, t]
    north = lambda v: pltpu.roll(v, 1, 0)
    south = lambda v: pltpu.roll(v, 23, 0)
    west = lambda v: pltpu.roll(v, 1, 1)
    east = lambda v: pltpu.roll(v, LANES - 1, 1)
    for step in range(2):

        @pl.loop(1, DEPTH + 1)
        def _(t):
            s = [cells[3 + f, t] for f in range(6)]
            below, above = cells[S11, t + 1], (cells[S12, t - 1], cells[S13, t - 1])
            new = velocities([cells[a, t] for a in range(3)], s, Q * mats[0, t - 1], below, above, north, south, west, east)
            for a in range(3):
                cells[a, t] = new[a]

        @pl.loop(1, DEPTH + 1)
        def _(t):
            v = [cells[a, t] for a in range(3)]
            s = [cells[3 + f, t] for f in range(6)]
            below, above = (cells[1, t + 1], cells[2, t + 1]), cells[0, t - 1]
            new = stresses(s, v, Q * mats[1, t - 1], Q * mats[2, t - 1], below, above, north, south, west, east)
            if step == 0:
                for f in range(6):
                    cells[3 + f, t] = new[f]
            else:
                for f, x in enumerate(v + new):
                    plain[f, t - 1] = x[0:R]

    for move in moves:
        move.wait()


def velocities(v, s, qb, s11_below, above, north, south, west, east):
    s11, s22, s33, s23, s13, s12 = s
    return [
        v[0] + qb * (s11_below - s11 + (s12 - north(s12)) + (s13 - west(s13))),
        v[1] + qb * (south(s22) - s22 + (s12 - above[0]) + (s23 - west(s23))),
        v[2] + qb * (east(s33) - s33 + (s13 - above[1]) + (s23 - north(s23))),
    ]


def stresses(s, v, la, m, below, v1_above, north, south, west, east):
    v1, v2, v3 = v
    d1, d2, d3 = v1 - v1_above, v2 - north(v2), v3 - west(v3)
    dil = la * (d1 + d2 + d3)
    m2 = 2.0 * m
    return [
        s[0] + (dil + m2 * d1),
        s[1] + (dil + m2 * d2),
        s[2] + (dil + m2 * d3),
        s[3] + m * (east(v2) - v2 + (south(v3) - v3)),
        s[4] + m * (east(v1) - v1 + (below[1] - v3)),
        s[5] + m * (south(v1) - v1 + (below[0] - v2)),
    ]


def final_kernel(filters, plain, seas, windows, last, recv, slab_out, ocean_out, flat, held, slab, sem):
    sec, me = lax.axis_index("sec"), lax.axis_index("blk")
    n_sec, n_blk = lax.axis_size("sec"), lax.axis_size("blk")
    shape = (32, LANES)
    lane, row = lane_iota(shape), row_iota(shape)
    before, after = jnp.maximum(me - 1, 0), jnp.minimum(me + 1, n_blk - 1)
    west_on, east_on = me > 0, me < n_blk - 1
    tile = (8, LANES)
    tlane = lane_iota(tile)

    moves = filter_moves(filters, held, sem)
    for move in moves:
        move.start()

    spot = tlane % SPAN
    north = lambda v: pltpu.roll(v, 1, 0)
    south = lambda v: pltpu.roll(v, 23, 0)
    west = lambda v: pltpu.roll(v, 1, 1)
    east = lambda v: pltpu.roll(v, LANES - 1, 1)
    wlane = lane_iota((24, LANES))
    above = lambda v: jnp.where(wlane < SPAN, 0.0, pltpu.roll(v, SPAN, 1))
    below = lambda v: jnp.where(wlane >= LANES - SPAN, 0.0, pltpu.roll(v, LANES - SPAN, 1))
    results = []
    for side in range(2):
        other, on, home = ((before, west_on, 6), (after, east_on, 8))[side]
        here = (spot >= home) & (spot < home + 2)
        state = []
        for f in range(12):
            parts = []
            for r in range(3):
                i = f * 3 + r
                x = pltpu.roll(recv[other, B_SLAB + i // 8], (home - 2 * (i % 8)) % LANES, 1)
                own = windows[f, 8 * r : 8 * r + 8, :] if r < 2 else last[f]
                parts.append(jnp.where(here, jnp.where(on, x, 0.0), own))
            state.append(jnp.concatenate(parts, axis=0))
        v, s = state[0:3], state[3:9]
        qb, la, m = Q * state[BUO], Q * state[LAM], Q * state[MU]
        for step in range(2):
            v = velocities(v, s, qb, below(s[0]), (above(s[5]), above(s[4])), north, south, west, east)
            s = stresses(s, v, la, m, (below(v[1]), below(v[2])), above(v[0]), north, south, west, east)
        results.append(v + s)
    edge = (tlane < 2) | (tlane >= LANES - 2)
    for f in range(9):
        for r in range(2):
            rows = slice(8 * r, 8 * r + 8)
            both = jnp.where(spot >= 8, results[0][f][rows], results[1][f][rows])
            for t in range(DEPTH):
                moved = pltpu.roll(both, (2 * LANES - SPAN * t - 8) % LANES, 1)
                slab[f, t, rows, :] = jnp.where(edge, moved, plain[f, t, rows, :])
    leave = pltpu.make_async_copy(slab, slab_out, sem.at[4])
    leave.start()

    rises = [jnp.concatenate([recv[j, B_UP + r] for r in range(4)], axis=0) for j in range(n_blk)]
    factors = []
    for j in range(n_blk):
        x = jnp.concatenate([recv[j, B_FACTOR], recv[j, B_FACTOR + 1]], axis=0)
        factors.append(jnp.concatenate([x, pltpu.roll(x, 64, 1)], axis=0))
    for j in range(n_blk - 1):
        terms = factors[j] * pltpu.roll(factors[j + 1], LANES - 32, 1)
        pick = lambda a, z: jnp.sum(jnp.where((lane >= a) & (lane < z), terms, 0.0), axis=1, keepdims=True)
        rises[j] = rises[j] + jnp.where(lane == LANES - 1, pick(0, 4), 0.0)
        rises[j + 1] = rises[j + 1] + jnp.where(lane == 0, pick(4, 21), 0.0) + jnp.where(lane == 1, pick(21, 22), 0.0)
    rise = jnp.concatenate(rises, axis=1)
    rise_hi = rise.astype(BF16).astype(F32)
    rise_lo = rise - rise_hi
    wide = row_iota(rise.shape)
    upper, lower = [], []
    for k in range(3):
        mine = (wide >= (0, 8, 24)[k]) & (wide < (8, 24, 32)[k])
        part = jnp.where(mine, rise_hi, 0.0)
        upper.append(jnp.concatenate([part, jnp.where(mine, rise_lo, 0.0)], axis=0))
        lower.append(jnp.concatenate([part, jnp.zeros_like(part)], axis=0))
    both = jnp.concatenate(upper + lower, axis=1).astype(BF16)
    flat[4 * LANES :, :] = jnp.zeros((LANES, LANES), F32)
    for k in range(4):
        moves[k].wait()
        rows = slice(k * LANES, (k + 1) * LANES + (16 if k == 3 else 0))
        part = lax.dot_general(held[rows, :], both, (((1,), (1,)), ((), ())), preferred_element_type=F32)
        flat[k * LANES : (k + 1) * LANES, 0:64] = part[0:LANES]
    flat[COLS : COLS + 8, 0:64] = part[LANES : LANES + 8]
    flat[5 * LANES - 8 : 5 * LANES, 0:64] = part[LANES + 8 : LANES + 16]
    turned = [flat[k * LANES : (k + 1) * LANES, :].T for k in range(5)]
    source = jnp.concatenate([x[0:32] + x[32:64] for x in turned], axis=1)

    ring = (32, 5 * LANES)
    fields = []
    for f in range(4):
        halo = []
        for r in range(4):
            at = 32 * f + 8 * r
            east_in = pltpu.roll(recv[after, B_OCEAN], (LANES - at) % LANES, 1)
            west_in = pltpu.roll(recv[before, B_OCEAN], (2 * LANES - 8 - at) % LANES, 1)
            x = jnp.where((tlane < 8) & east_on, east_in, 0.0)
            halo.append(jnp.where((tlane >= LANES - 8) & west_on, west_in, x))
        fields.append(jnp.concatenate([seas[f], jnp.concatenate(halo, axis=0)], axis=1))
    surface, strike, dip, water = fields
    at = lane_iota(ring)
    at = jnp.where(at >= 5 * LANES - 8, at - 5 * LANES, at)
    x, y = row_iota(ring) - 8 + sec * R, at + me * COLS
    wet = (x >= 0) & (x < n_sec * R) & (y >= 0) & (y < n_blk * COLS) & (at < COLS + 8)
    surface = surface + source
    water = 0.25 * water
    for step in range(4):
        change = pltpu.roll(strike, 31, 0) - pltpu.roll(strike, 1, 0)
        change = change + (pltpu.roll(dip, 5 * LANES - 1, 1) - pltpu.roll(dip, 1, 1))
        surface = jnp.where(wet, surface - 0.25 * change, 0.0)
        strike = strike - water * (pltpu.roll(surface, 31, 0) - pltpu.roll(surface, 1, 0))
        dip = dip - water * (pltpu.roll(surface, 5 * LANES - 1, 1) - pltpu.roll(surface, 1, 1))
    ocean_out[0] = surface[8:24, 0:COLS]
    ocean_out[1] = strike[8:24, 0:COLS]
    ocean_out[2] = dip[8:24, 0:COLS]
    leave.wait()


def call(kernel, out_shape, flops, *args, far=0, out_far=(), limit=None, scratch=()):
    outs = list(out_shape)
    n_bytes = sum(a.size * a.dtype.itemsize for a in args) + sum(math.prod(o.shape) * o.dtype.itemsize for o in outs)
    anywhere = pl.BlockSpec(memory_space=pl.ANY)
    return pl.pallas_call(
        kernel,
        out_shape=out_shape,
        in_specs=[anywhere] * far + [VMEM] * (len(args) - far),
        out_specs=[anywhere if i in out_far else VMEM for i in range(len(outs))],
        scratch_shapes=scratch,
        compiler_params=pltpu.CompilerParams(vmem_limit_bytes=limit) if limit else None,
        cost_estimate=pl.CostEstimate(flops=flops, bytes_accessed=n_bytes, transcendentals=0),
    )(*args)


def swap(x, axis, start):
    pairs = []
    for i in range(start, lax.axis_size(axis) - 1, 2):
        pairs += [(i, i + 1), (i + 1, i)]
    return lax.ppermute(x, axis, pairs)


def on_device(slab_state, buoyancy, lame_lambda, lame_mu, face_map, band_widths, ocean_state, water_depth):
    n_blk = lax.axis_size("blk")
    n_face = face_map.shape[0]
    arr = jax.ShapeDtypeStruct
    own = (slab_state, buoyancy, lame_lambda, lame_mu, ocean_state, water_depth)
    message = arr((SEC_TILES, 8, LANES), F32)
    sources = (*own, band_widths)
    first, second = call(
        pack_kernel,
        [message, message],
        10**6,
        *sources,
        far=7,
        scratch=[pltpu.VMEM(a.shape, a.dtype) for a in sources] + [pltpu.SemaphoreType.DMA((7,))],
    )
    first = swap(first, "sec", 1)
    second = swap(second, "sec", 0)
    state, sea, windows, halos = call(
        carry_kernel,
        [
            arr((12, DEPTH, R, LANES), F32),
            arr((4, R, COLS), F32),
            arr((12, R, LANES), F32),
            arr((2, 5, 8, LANES), F32),
        ],
        10**7,
        *own,
        limit=MIB * 12,
    )
    send, strips, last = call(
        uplift_kernel,
        [
            arr((n_blk, BLK_TILES, 8, LANES), F32),
            arr((12, DEPTH, 8, LANES), F32),
            arr((12, 8, LANES), F32),
        ],
        10**7,
        state,
        sea,
        halos,
        first,
        second,
        limit=MIB * 12,
    )
    recv = lax.all_to_all(send, "blk", 0, 0, tiled=True)
    filters = arr((4 * (COLS + 16), 6 * n_face), BF16)
    plain, seas, filters = call(
        middle_kernel,
        [arr(slab_state.shape, F32), arr((4, 32, COLS), F32), filters],
        10**8,
        state,
        sea,
        first,
        second,
        strips,
        face_map.reshape(1, n_face),
        band_widths,
        out_far=(2,),
        limit=MIB * 46,
        scratch=[
            pltpu.VMEM((9, DEPTH + 2, 24, LANES), F32),
            pltpu.VMEM((3, DEPTH, 24, LANES), F32),
            pltpu.VMEM((COLS + 16, 6 * n_face), BF16),
            pltpu.SemaphoreType.DMA((4,)),
        ],
    )
    return call(
        final_kernel,
        [arr(slab_state.shape, F32), arr(ocean_state.shape, F32)],
        10**8,
        filters,
        plain,
        seas,
        windows,
        last,
        recv,
        far=1,
        out_far=(0,),
        limit=MIB * 46,
        scratch=[
            pltpu.VMEM((5 * LANES, LANES), F32),
            pltpu.VMEM((COLS + 16, 6 * n_face), BF16),
            pltpu.VMEM(slab_state.shape, F32),
            pltpu.SemaphoreType.DMA((5,)),
        ],
    )


def solution(mesh):
    in_specs = (
        P(None, None, "sec", "blk"),
        P(None, "sec", "blk"),
        P(None, "sec", "blk"),
        P(None, "sec", "blk"),
        P(),
        P("sec", None),
        P(None, "sec", "blk"),
        P("sec", "blk"),
    )
    out_specs = (P(None, None, "sec", "blk"), P(None, "sec", "blk"))
    return jax.shard_map(on_device, mesh=mesh, in_specs=in_specs, out_specs=out_specs, check_vma=False)
```

```python
import math

import jax
import jax.numpy as jnp
from jax import lax
from jax.experimental import pallas as pl
from jax.experimental.pallas import tpu as pltpu
from jax.sharding import PartitionSpec as P

Q = 0.25
R = 16
LANES = 128
DEPTH = 8
COLS = 512
S11, S22, S33, S23, S13, S12, BUO, LAM, MU = 3, 4, 5, 6, 7, 8, 9, 10, 11
UP_PLANES = [(S11, 0), (S11, 1), (S11, 2)] + [
    (f, t) for f in (S12, S13, S23, S22, S33, 0, 1, 2, BUO, LAM, MU) for t in (0, 1)
]
N_UP = len(UP_PLANES)
UP_INDEX = {ft: i for i, ft in enumerate(UP_PLANES)}
REST = [(f, t) for f in range(12) for t in range(DEPTH) if (f, t) not in UP_INDEX]
STRIP = N_UP
MISC = STRIP + (len(REST) + 3) // 4
OCEAN = MISC + 1
SEC_TILES = OCEAN + 16
B_UP, B_FACTOR, B_SLAB, B_OCEAN, BLK_TILES = 0, 4, 6, 11, 12
SPAN = 16
F32 = jnp.float32
MIB = 1 << 20
PAD = 36
BF16 = jnp.bfloat16
VMEM = pl.BlockSpec(memory_space=pltpu.VMEM)


def lane_iota(shape):
    return lax.broadcasted_iota(jnp.int32, shape, len(shape) - 1)


def row_iota(shape):
    return lax.broadcasted_iota(jnp.int32, shape, 0)


def fetch(sources, targets, sem, others):
    moves = [pltpu.make_async_copy(a, b, sem.at[i]) for i, (a, b) in enumerate(zip(sources, targets))]
    for move in moves + others:
        move.start()
    for move in moves:
        move.wait()


def pack_kernel(*refs):
    sources, (first, second, state, sea), copies, sem, join_sem = refs[:7], refs[7:11], refs[11:18], refs[18], refs[19]
    parts = [state.at[0:9], state.at[9], state.at[10], state.at[11], sea.at[0:3], sea.at[3]]
    joins = [pltpu.make_async_copy(a, b, join_sem.at[i]) for i, (a, b) in enumerate(zip(sources, parts))]
    fetch(sources, copies, sem, joins)
    widths = copies[6]
    slab, buo, lam, mu, ocean, depth = copies[:6]
    odd = lax.rem(lax.axis_index("sec"), 2)

    def read(f, t, rows):
        return slab[f, t, rows, :] if f < 9 else (buo, lam, mu)[f - 9][t, rows, :]

    for out, lower in ((first, odd), (second, 1 - odd)):
        start = pl.multiple_of(lower * 8, 8)
        rows = pl.ds(start, 8)
        for i, (f, t) in enumerate(UP_PLANES):
            out[i] = read(f, t, rows)
        out[MISC - 1] = jnp.zeros((8, LANES), F32)
        for p, (f, t) in enumerate(REST):
            strip = jnp.where(lower == 1, read(f, t, slice(14, 16)), read(f, t, slice(0, 2)))
            out[STRIP + p // 4, 2 * (p % 4) : 2 * (p % 4) + 2, :] = strip
        out[MISC] = jnp.zeros((8, LANES), F32)
        for t in (0, 1):
            out[MISC, t : t + 1, :] = read(S12, t, slice(7, 8))
        out[MISC, 2:3, 0 : widths.shape[1]] = widths[...].astype(F32)
        for f in range(4):
            for k in range(4):
                cols = slice(k * LANES, (k + 1) * LANES)
                out[OCEAN + 4 * f + k] = ocean[f, rows, cols] if f < 3 else depth[rows, cols]
    for join in joins:
        join.wait()


def sides(first, second):
    odd = lax.rem(lax.axis_index("sec"), 2)

    def top(i):
        return jnp.where(odd == 0, first[i], second[i])

    def bottom(i):
        return jnp.where(odd == 0, second[i], first[i])

    return top, bottom


def edges(x, r, tlane):
    out = None
    for t in range(DEPTH):
        moved = pltpu.roll(x[t, 8 * r : 8 * r + 8], (SPAN * t + 8) % LANES, 1)
        out = moved if t == 0 else jnp.where(tlane >= SPAN * t, moved, out)
    return out


def fill_strips(strips, first, second):
    top, bottom = sides(first, second)
    odd = lax.rem(lax.axis_index("sec"), 2)
    row = row_iota((8, LANES))
    for i, (f, t) in enumerate(UP_PLANES):
        strips[f, t] = jnp.where(row < 2, bottom(i), jnp.where(row >= 6, top(i), 0.0))
    for p, (f, t) in enumerate(REST):
        i, at = STRIP + p // 4, slice(2 * (p % 4), 2 * (p % 4) + 2)
        a, c = first[i, at, :], second[i, at, :]
        strips[f, t] = jnp.zeros((8, LANES), F32)
        strips[f, t, 0:2, :] = jnp.where(odd == 0, c, a)
        strips[f, t, 6:8, :] = jnp.where(odd == 0, a, c)


def halo_spot(f, r, tlane):
    i = f * 3 + r
    at = 2 * (i % 8)
    spot = tlane % SPAN
    return i // 8, at, (spot >= at) & (spot < at + 2)


def carry_kernel(state_in, sea_in, state, sea, windows, halos):
    state[...] = state_in[...]
    sea[...] = sea_in[...]
    tlane = lane_iota((8, LANES))
    heads = [jnp.zeros((8, LANES), F32) for _ in range(5)]
    tails = [jnp.zeros((8, LANES), F32) for _ in range(5)]
    for f in range(12):
        for r in range(2):
            x = edges(state_in.at[f], r, tlane)
            windows[f, 8 * r : 8 * r + 8, :] = x
            k, at, here = halo_spot(f, r, tlane)
            heads[k] = jnp.where(here, pltpu.roll(x, (at - 8) % LANES, 1), heads[k])
            tails[k] = jnp.where(here, pltpu.roll(x, (at - 6) % LANES, 1), tails[k])
    for k in range(5):
        halos[0, k] = heads[k]
        halos[1, k] = tails[k]


def uplift_kernel(state, sea, halos, first, second, send, last, strips):
    me = lax.axis_index("blk")
    top, bottom = sides(first, second)
    shape = (32, LANES)
    lane, row = lane_iota(shape), row_iota(shape)

    def plane(f, t):
        i = UP_INDEX[(f, t)]
        return jnp.concatenate([top(i), state[f, t], bottom(i)], axis=0)

    def north(x):
        return pltpu.roll(x, 1, 0)

    def south(x):
        return pltpu.roll(x, 31, 0)

    def west(x):
        return jnp.where(lane == 0, 0.0, pltpu.roll(x, 1, 1))

    def east(x):
        return jnp.where(lane == LANES - 1, 0.0, pltpu.roll(x, LANES - 1, 1))

    s11 = [plane(S11, t) for t in range(3)]
    s22, s33, s23, s13, s12 = ([plane(f, t) for t in (0, 1)] for f in (S22, S33, S23, S13, S12))
    b, la, m = ([plane(f, t) for t in (0, 1)] for f in (BUO, LAM, MU))
    misc = top(MISC)
    v1, v2, v3 = [], [], []
    for t in (0, 1):
        above = lambda s: s[t] - s[t - 1] if t else s[t]
        s12n = jnp.where(row == 0, misc[t : t + 1, :], north(s12[t]))
        v1.append(plane(0, t) + Q * b[t] * (s11[t + 1] - s11[t] + (s12[t] - s12n) + (s13[t] - west(s13[t]))))
        v2.append(plane(1, t) + Q * b[t] * (south(s22[t]) - s22[t] + above(s12) + (s23[t] - west(s23[t]))))
        v3.append(plane(2, t) + Q * b[t] * (east(s33[t]) - s33[t] + above(s13) + (s23[t] - north(s23[t]))))
    n11 = []
    for t in (0, 1):
        d1 = v1[t] - v1[t - 1] if t else v1[t]
        dil = d1 + (v2[t] - north(v2[t])) + (v3[t] - west(v3[t]))
        n11.append(s11[t] + Q * (la[t] * dil + 2.0 * m[t] * d1))
    n12 = s12[0] + Q * m[0] * (south(v1[0]) - v1[0] + v2[1] - v2[0])
    n13 = s13[0] + Q * m[0] * (east(v1[0]) - v1[0] + v3[1] - v3[0])
    g = Q * Q * b[0]
    rise = 2.0 * Q * v1[0] + g * (n11[1] - n11[0] + n12 - north(n12) + n13 - west(n13))

    la0, la1 = Q * la[0], Q * la[1]
    m0, m1 = la0 + 2.0 * Q * m[0], la1 + 2.0 * Q * m[1]
    q0 = Q * m[0]
    q0n = north(q0)
    b0, b1 = Q * b[0], Q * b[1]
    left = [
        g * (la1 + q0) * b1,
        -g * (la0 + q0) * b0,
        g * q0,
        g * q0 * s13[0],
        s13[0],
        south(s13[0]),
        north(s13[0]),
        s13[1],
        s23[0],
        north(s23[0]),
        s23[1],
        north(s23[1]),
        v3[1],
        b1,
        v3[0],
        b0,
        n13,
        q0,
        q0 * s13[0],
        q0 * b1,
        q0 * b0,
        s13[0],
    ]
    right = [
        s33[1],
        s33[0],
        v1[0],
        -b0,
        -(2.0 * Q - g * (m1 + m0 + 2.0 * q0 + q0n)) * b0,
        -g * q0 * south(b0),
        -g * q0n * north(b0),
        -g * m1 * b1,
        g * (la0 + q0) * b0,
        -g * (la0 + q0n) * north(b0),
        -g * (la1 + q0) * b1,
        g * (la1 + q0n) * north(b1),
        -g * la1,
        -g * la1 * s33[1],
        g * la0,
        g * la0 * s33[0],
        -g,
        -g * v1[0],
        g * b0,
        -g * s33[1],
        g * s33[0],
        -pltpu.roll(g, LANES - 1, 1) * q0 * b0,
    ]
    factors = jnp.zeros(shape, F32)
    for i, (x, y) in enumerate(zip(left, right)):
        factors = jnp.where(lane == i, pltpu.roll(x, (i + 1) % LANES, 1), factors)
        factors = jnp.where(lane == 32 + i, pltpu.roll(y, 32 + i, 1), factors)
    packed = jnp.where(lane[:16] < 64, factors[:16], pltpu.roll(factors[16:], 64, 1))

    tile = (8, LANES)
    tlane = lane_iota(tile)
    fill_strips(strips, first, second)
    heads = [halos[0, k] for k in range(5)]
    tails = [halos[1, k] for k in range(5)]
    for f in range(12):
        x = edges(strips.at[f], 0, tlane)
        last[f] = x
        k, at, here = halo_spot(f, 2, tlane)
        heads[k] = jnp.where(here, pltpu.roll(x, (at - 8) % LANES, 1), heads[k])
        tails[k] = jnp.where(here, pltpu.roll(x, (at - 6) % LANES, 1), tails[k])
    head, tail = jnp.zeros(tile, F32), jnp.zeros(tile, F32)
    for f in range(4):
        for r in range(4):
            at = 32 * f + 8 * r
            ends = []
            for k in (0, 3):
                cols = slice(k * LANES, (k + 1) * LANES)
                rows = slice(8 * r - 8, 8 * r)
                if r == 0:
                    x = top(OCEAN + 4 * f + k)
                elif r == 3:
                    x = bottom(OCEAN + 4 * f + k)
                else:
                    x = sea[f, rows, cols]
                ends.append(x)
            here = (tlane >= at) & (tlane < at + 8)
            head = jnp.where(here, pltpu.roll(ends[0], at, 1), head)
            tail = jnp.where(here, pltpu.roll(ends[1], (at + 8) % LANES, 1), tail)
    heads.append(head)
    tails.append(tail)
    for d in range(send.shape[0]):
        for r in range(4):
            send[d, B_UP + r] = rise[8 * r : 8 * r + 8]
        for r in range(2):
            send[d, B_FACTOR + r] = packed[8 * r : 8 * r + 8]
        for i in range(6):
            send[d, B_SLAB + i] = jnp.where(d < me, heads[i], tails[i])


def filter_moves(source, target, sem):
    rows = [slice(k * LANES, (k + 1) * LANES + (16 if k == 3 else 0)) for k in range(4)]
    return [pltpu.make_async_copy(source.at[at, :], target.at[at, :], sem.at[k]) for k, at in enumerate(rows)]


def middle_kernel(
    state, sea, first, second, face, widths, plain_out, near, far, cells, mats, held, strips, plain, sem
):
    me = lax.axis_index("blk")
    top, bottom = sides(first, second)
    lane = lane_iota((1, LANES))
    face_at = (face[...] - me * COLS).astype(F32)
    width = face.shape[1]

    def scales(row):
        out = []
        for j in (me, me + 1, me - 1):
            w = jnp.sum(jnp.where(lane[:, : row.shape[1]] == j, row, 0.0), axis=1, keepdims=True)
            w = jnp.where(w > 0.0, w, 1.0)
            out.append((-(math.pi / 2.0) * math.log2(math.e) / w, 1.0 / w))
        return out

    groups = [scales(top(MISC)[2:3, :]), scales(widths[...].astype(F32)), scales(bottom(MISC)[2:3, :])]

    def put(k, rows, distance, rate, gain):
        decay = jnp.exp2(distance * rate)
        value = decay / (1.0 + decay * decay) * gain
        upper = value.astype(BF16)
        out, at = (near, 0) if k == 1 else (held, k * width)
        out[rows, at : at + width] = upper
        out[rows, at + width : at + 2 * width] = (value - upper.astype(F32)).astype(BF16)

    row = row_iota((16, width))
    at = jnp.where(row < 8, row + COLS, row - 16).astype(F32)
    distance = jnp.abs(at - face_at)
    for k in range(3):
        rate = jnp.where(row < 8, groups[k][1][0], groups[k][2][0])
        gain = jnp.where(row < 8, groups[k][1][1], groups[k][2][1])
        put(k, slice(COLS, COLS + 16), distance, rate, gain)
    moves = filter_moves(held, far, sem)
    for piece in range(4):

        @pl.loop(piece * LANES // 16, (piece + 1) * LANES // 16)
        def _(c):
            start = pl.multiple_of(c * 16, 16)
            at = (lax.broadcasted_iota(jnp.int32, (16, width), 0) + start).astype(F32)
            distance = jnp.abs(at - face_at)
            for k in range(3):
                put(k, pl.ds(start, 16), distance, *groups[k][0])

        moves[piece].start()

    for f in range(4):
        for k in range(4):
            cols = slice(k * LANES, (k + 1) * LANES)
            i = OCEAN + 4 * f + k
            plain[9 + f, 2 * k, 0:8, :] = top(i)
            plain[9 + f, 2 * k, 8:16, :] = sea[f, 0:8, cols]
            plain[9 + f, 2 * k + 1, 0:8, :] = sea[f, 8:16, cols]
            plain[9 + f, 2 * k + 1, 8:16, :] = bottom(i)

    fill_strips(strips, first, second)
    for f in range(9):
        for t in (0, DEPTH + 1):
            cells[f, t] = jnp.zeros((24, LANES), F32)
    for f in range(12):
        for t in range(DEPTH):
            if f < 9:
                cells[f, t + 1, 0:R, :] = state[f, t]
                cells[f, t + 1, R:, :] = strips[f, t]
            else:
                mats[f - 9, t, 0:R, :] = state[f, t]
                mats[f - 9, t, R:, :] = strips[f, t]
    north = lambda v: pltpu.roll(v, 1, 0)
    south = lambda v: pltpu.roll(v, 23, 0)
    west = lambda v: pltpu.roll(v, 1, 1)
    east = lambda v: pltpu.roll(v, LANES - 1, 1)
    for step in range(2):

        @pl.loop(1, DEPTH + 1)
        def _(t):
            s = [cells[3 + f, t] for f in range(6)]
            below, above = cells[S11, t + 1], (cells[S12, t - 1], cells[S13, t - 1])
            new = velocities([cells[a, t] for a in range(3)], s, Q * mats[0, t - 1], below, above, north, south, west, east)
            for a in range(3):
                cells[a, t] = new[a]

        @pl.loop(1, DEPTH + 1)
        def _(t):
            v = [cells[a, t] for a in range(3)]
            s = [cells[3 + f, t] for f in range(6)]
            below, above = (cells[1, t + 1], cells[2, t + 1]), cells[0, t - 1]
            new = stresses(s, v, Q * mats[1, t - 1], Q * mats[2, t - 1], below, above, north, south, west, east)
            if step == 0:
                for f in range(6):
                    cells[3 + f, t] = new[f]
            else:
                for f, x in enumerate(v + new):
                    plain[f, t - 1] = x[0:R]

    leave = pltpu.make_async_copy(plain, plain_out.at[0:13], sem.at[4])
    leave.start()
    for move in moves + [leave]:
        move.wait()


def velocities(v, s, qb, s11_below, above, north, south, west, east):
    s11, s22, s33, s23, s13, s12 = s
    return [
        v[0] + qb * (s11_below - s11 + (s12 - north(s12)) + (s13 - west(s13))),
        v[1] + qb * (south(s22) - s22 + (s12 - above[0]) + (s23 - west(s23))),
        v[2] + qb * (east(s33) - s33 + (s13 - above[1]) + (s23 - north(s23))),
    ]


def stresses(s, v, la, m, below, v1_above, north, south, west, east):
    v1, v2, v3 = v
    d1, d2, d3 = v1 - v1_above, v2 - north(v2), v3 - west(v3)
    dil = la * (d1 + d2 + d3)
    m2 = 2.0 * m
    return [
        s[0] + (dil + m2 * d1),
        s[1] + (dil + m2 * d2),
        s[2] + (dil + m2 * d3),
        s[3] + m * (east(v2) - v2 + (south(v3) - v3)),
        s[4] + m * (east(v1) - v1 + (below[1] - v3)),
        s[5] + m * (south(v1) - v1 + (below[0] - v2)),
    ]


def final_kernel(far, plain_in, near, windows, last, recv, slab_out, ocean_out, flat, held, plain, slab, sem):
    sec, me = lax.axis_index("sec"), lax.axis_index("blk")
    n_sec, n_blk = lax.axis_size("sec"), lax.axis_size("blk")
    shape = (32, LANES)
    lane, row = lane_iota(shape), row_iota(shape)
    before, after = jnp.maximum(me - 1, 0), jnp.minimum(me + 1, n_blk - 1)
    west_on, east_on = me > 0, me < n_blk - 1
    tile = (8, LANES)
    tlane = lane_iota(tile)

    enter = pltpu.make_async_copy(plain_in.at[0:13], plain, sem.at[5])
    moves = filter_moves(far, held, sem)
    for move in [enter] + moves:
        move.start()

    spot = tlane % SPAN
    north = lambda v: pltpu.roll(v, 1, 0)
    south = lambda v: pltpu.roll(v, 23, 0)
    west = lambda v: pltpu.roll(v, 1, 1)
    east = lambda v: pltpu.roll(v, LANES - 1, 1)
    wlane = lane_iota((24, LANES))
    above = lambda v: jnp.where(wlane < SPAN, 0.0, pltpu.roll(v, SPAN, 1))
    below = lambda v: jnp.where(wlane >= LANES - SPAN, 0.0, pltpu.roll(v, LANES - SPAN, 1))
    results = []
    for side in range(2):
        other, on, home = ((before, west_on, 6), (after, east_on, 8))[side]
        here = (spot >= home) & (spot < home + 2)
        state = []
        for f in range(12):
            parts = []
            for r in range(3):
                i = f * 3 + r
                x = pltpu.roll(recv[other, B_SLAB + i // 8], (home - 2 * (i % 8)) % LANES, 1)
                own = windows[f, 8 * r : 8 * r + 8, :] if r < 2 else last[f]
                parts.append(jnp.where(here, jnp.where(on, x, 0.0), own))
            state.append(jnp.concatenate(parts, axis=0))
        v, s = state[0:3], state[3:9]
        qb, la, m = Q * state[BUO], Q * state[LAM], Q * state[MU]
        for step in range(2):
            v = velocities(v, s, qb, below(s[0]), (above(s[5]), above(s[4])), north, south, west, east)
            s = stresses(s, v, la, m, (below(v[1]), below(v[2])), above(v[0]), north, south, west, east)
        results.append(v + s)
    enter.wait()
    edge = (tlane < 2) | (tlane >= LANES - 2)
    for f in range(9):
        for r in range(2):
            rows = slice(8 * r, 8 * r + 8)
            both = jnp.where(spot >= 8, results[0][f][rows], results[1][f][rows])
            for t in range(DEPTH):
                moved = pltpu.roll(both, (2 * LANES - SPAN * t - 8) % LANES, 1)
                slab[f, t, rows, :] = jnp.where(edge, moved, plain[f, t, rows, :])
    leave = pltpu.make_async_copy(slab, slab_out, sem.at[4])
    leave.start()

    rises = [jnp.concatenate([recv[j, B_UP + r] for r in range(4)], axis=0) for j in range(n_blk)]
    factors = []
    for j in range(n_blk):
        x = jnp.concatenate([recv[j, B_FACTOR], recv[j, B_FACTOR + 1]], axis=0)
        factors.append(jnp.concatenate([x, pltpu.roll(x, 64, 1)], axis=0))
    for j in range(n_blk - 1):
        terms = factors[j] * pltpu.roll(factors[j + 1], LANES - 32, 1)
        pick = lambda a, z: jnp.sum(jnp.where((lane >= a) & (lane < z), terms, 0.0), axis=1, keepdims=True)
        rises[j] = rises[j] + jnp.where(lane == LANES - 1, pick(0, 4), 0.0)
        rises[j + 1] = rises[j + 1] + jnp.where(lane == 0, pick(4, 21), 0.0) + jnp.where(lane == 1, pick(21, 22), 0.0)
    rise = jnp.concatenate(rises, axis=1)
    rise_hi = rise.astype(BF16).astype(F32)
    rise_lo = rise - rise_hi
    wide = row_iota(rise.shape)
    upper = {}
    for k in (1, 0, 2):
        mine = (wide >= (0, 8, 24)[k]) & (wide < (8, 24, 32)[k])
        part = jnp.where(mine, rise_hi, 0.0)
        upper[k] = jnp.concatenate([part, jnp.where(mine, rise_lo, 0.0)], axis=0).astype(BF16)
        upper[k] = [upper[k], jnp.concatenate([part, jnp.zeros_like(part)], axis=0).astype(BF16)]

    def dot(a, c):
        return lax.dot_general(a, c, (((1,), (1,)), ((), ())), preferred_element_type=F32)

    for move in moves:
        move.wait()
    source = dot(near[...], jnp.concatenate(upper[1], axis=1))
    source = source + dot(held[...], jnp.concatenate(upper[0] + upper[2], axis=1))
    flat[4 * LANES :, :] = jnp.zeros((LANES, LANES), F32)
    flat[0 : COLS + 8, 0:64] = source[0 : COLS + 8]
    flat[5 * LANES - 8 : 5 * LANES, 0:64] = source[COLS + 8 : COLS + 16]
    turned = [flat[k * LANES : (k + 1) * LANES, :].T for k in range(5)]
    source = jnp.concatenate([x[0:32] + x[32:64] for x in turned], axis=1)

    ring = (32, 5 * LANES)
    fields = []
    for f in range(4):
        halo = []
        for r in range(4):
            at = 32 * f + 8 * r
            east_in = pltpu.roll(recv[after, B_OCEAN], (LANES - at) % LANES, 1)
            west_in = pltpu.roll(recv[before, B_OCEAN], (2 * LANES - 8 - at) % LANES, 1)
            x = jnp.where((tlane < 8) & east_on, east_in, 0.0)
            halo.append(jnp.where((tlane >= LANES - 8) & west_on, west_in, x))
        tiles = [jnp.concatenate([plain[9 + f, 2 * k], plain[9 + f, 2 * k + 1]], axis=0) for k in range(4)]
        fields.append(jnp.concatenate(tiles + [jnp.concatenate(halo, axis=0)], axis=1))
    surface, strike, dip, water = fields
    at = lane_iota(ring)
    at = jnp.where(at >= 5 * LANES - 8, at - 5 * LANES, at)
    x, y = row_iota(ring) - 8 + sec * R, at + me * COLS
    wet = (x >= 0) & (x < n_sec * R) & (y >= 0) & (y < n_blk * COLS) & (at < COLS + 8)
    surface = surface + source
    water = 0.25 * water
    for step in range(4):
        change = pltpu.roll(strike, 31, 0) - pltpu.roll(strike, 1, 0)
        change = change + (pltpu.roll(dip, 5 * LANES - 1, 1) - pltpu.roll(dip, 1, 1))
        surface = jnp.where(wet, surface - 0.25 * change, 0.0)
        strike = strike - water * (pltpu.roll(surface, 31, 0) - pltpu.roll(surface, 1, 0))
        dip = dip - water * (pltpu.roll(surface, 5 * LANES - 1, 1) - pltpu.roll(surface, 1, 1))
    ocean_out[0] = surface[8:24, 0:COLS]
    ocean_out[1] = strike[8:24, 0:COLS]
    ocean_out[2] = dip[8:24, 0:COLS]
    leave.wait()


def call(kernel, out_shape, flops, *args, far=0, out_far=(), limit=None, scratch=()):
    outs = list(out_shape)
    n_bytes = sum(a.size * a.dtype.itemsize for a in args) + sum(math.prod(o.shape) * o.dtype.itemsize for o in outs)
    anywhere = pl.BlockSpec(memory_space=pl.ANY)
    return pl.pallas_call(
        kernel,
        out_shape=out_shape,
        in_specs=[anywhere] * far + [VMEM] * (len(args) - far),
        out_specs=[anywhere if i in out_far else VMEM for i in range(len(outs))],
        scratch_shapes=scratch,
        compiler_params=pltpu.CompilerParams(vmem_limit_bytes=limit) if limit else None,
        cost_estimate=pl.CostEstimate(flops=flops, bytes_accessed=n_bytes, transcendentals=0),
    )(*args)


def swap(x, axis, start):
    pairs = []
    for i in range(start, lax.axis_size(axis) - 1, 2):
        pairs += [(i, i + 1), (i + 1, i)]
    return lax.ppermute(x, axis, pairs)


def on_device(slab_state, buoyancy, lame_lambda, lame_mu, face_map, band_widths, ocean_state, water_depth):
    n_blk = lax.axis_size("blk")
    n_face = face_map.shape[0]
    arr = jax.ShapeDtypeStruct
    own = (slab_state, buoyancy, lame_lambda, lame_mu, ocean_state, water_depth)
    message = arr((SEC_TILES, 8, LANES), F32)
    sources = (*own, band_widths)
    state, sea = arr((12, DEPTH, R, LANES), F32), arr((4, R, COLS), F32)
    first, second, state, sea = call(
        pack_kernel,
        [message, message, state, sea],
        10**6,
        *sources,
        far=7,
        out_far=(2, 3),
        scratch=[pltpu.VMEM(a.shape, a.dtype) for a in sources]
        + [pltpu.SemaphoreType.DMA((7,)), pltpu.SemaphoreType.DMA((6,))],
    )
    first = swap(first, "sec", 1)
    second = swap(second, "sec", 0)
    state, sea, windows, halos = call(
        carry_kernel,
        [
            arr(state.shape, F32),
            arr(sea.shape, F32),
            arr((12, R, LANES), F32),
            arr((2, 5, 8, LANES), F32),
        ],
        10**7,
        state,
        sea,
        limit=MIB * 12,
    )
    strips = pltpu.VMEM((12, DEPTH, 8, LANES), F32)
    send, last = call(
        uplift_kernel,
        [arr((n_blk, BLK_TILES, 8, LANES), F32), arr((12, 8, LANES), F32)],
        10**7,
        state,
        sea,
        halos,
        first,
        second,
        limit=MIB * 12,
        scratch=[strips],
    )
    recv = lax.all_to_all(send, "blk", 0, 0, tiled=True)
    near = arr((COLS + 16, 2 * n_face), BF16)
    far = arr((6 * (COLS + 16), 4 * n_face), BF16)
    held = pltpu.VMEM((COLS + 16, 4 * n_face), BF16)
    plain = arr((PAD * 9, *slab_state.shape[1:]), F32)
    plain, near, far = call(
        middle_kernel,
        [plain, near, far],
        10**8,
        state,
        sea,
        first,
        second,
        face_map.reshape(1, n_face),
        band_widths,
        out_far=(0, 2),
        limit=MIB * 46,
        scratch=[
            pltpu.VMEM((9, DEPTH + 2, 24, LANES), F32),
            pltpu.VMEM((3, DEPTH, 24, LANES), F32),
            held,
            strips,
            pltpu.VMEM((13, DEPTH, R, LANES), F32),
            pltpu.SemaphoreType.DMA((5,)),
        ],
    )
    return call(
        final_kernel,
        [arr(slab_state.shape, F32), arr(ocean_state.shape, F32)],
        10**8,
        far,
        plain,
        near,
        windows,
        last,
        recv,
        far=2,
        out_far=(0,),
        limit=MIB * 46,
        scratch=[
            pltpu.VMEM((5 * LANES, LANES), F32),
            held,
            pltpu.VMEM((13, DEPTH, R, LANES), F32),
            pltpu.VMEM(slab_state.shape, F32),
            pltpu.SemaphoreType.DMA((6,)),
        ],
    )


def solution(mesh):
    in_specs = (
        P(None, None, "sec", "blk"),
        P(None, "sec", "blk"),
        P(None, "sec", "blk"),
        P(None, "sec", "blk"),
        P(),
        P("sec", None),
        P(None, "sec", "blk"),
        P("sec", "blk"),
    )
    out_specs = (P(None, None, "sec", "blk"), P(None, "sec", "blk"))
    return jax.shard_map(on_device, mesh=mesh, in_specs=in_specs, out_specs=out_specs, check_vma=False)
```

```python
import math

import jax
import jax.numpy as jnp
from jax import lax
from jax.experimental import pallas as pl
from jax.experimental.pallas import tpu as pltpu
from jax.sharding import PartitionSpec as P

Q = 0.25
R = 16
LANES = 128
DEPTH = 8
COLS = 512
S11, S22, S33, S23, S13, S12, BUO, LAM, MU = 3, 4, 5, 6, 7, 8, 9, 10, 11
UP_PLANES = [(S11, 0), (S11, 1), (S11, 2)] + [
    (f, t) for f in (S12, S13, S23, S22, S33, 0, 1, 2, BUO, LAM, MU) for t in (0, 1)
]
N_UP = len(UP_PLANES)
UP_INDEX = {ft: i for i, ft in enumerate(UP_PLANES)}
REST = [(f, t) for f in range(12) for t in range(DEPTH) if (f, t) not in UP_INDEX]
STRIP = N_UP
MISC = STRIP + (len(REST) + 3) // 4
OCEAN = MISC + 1
SEC_TILES = OCEAN + 16
B_UP, B_FACTOR, B_SLAB, B_OCEAN, BLK_TILES = 0, 4, 6, 10, 11
SPAN = 16
F32 = jnp.float32
MIB = 1 << 20
PAD = 36
BF16 = jnp.bfloat16
VMEM = pl.BlockSpec(memory_space=pltpu.VMEM)


def lane_iota(shape):
    return lax.broadcasted_iota(jnp.int32, shape, len(shape) - 1)


def row_iota(shape):
    return lax.broadcasted_iota(jnp.int32, shape, 0)


def fetch(sources, targets, sem):
    moves = [pltpu.make_async_copy(a, b, sem.at[i]) for i, (a, b) in enumerate(zip(sources, targets))]
    for move in moves:
        move.start()
    for move in moves:
        move.wait()


def pack_kernel(*refs):
    sources, (first, second), copies, sem = refs[:7], refs[7:9], refs[9:16], refs[16]
    fetch(sources, copies, sem)
    widths = copies[6]
    slab, buo, lam, mu, ocean, depth = copies[:6]
    odd = lax.rem(lax.axis_index("sec"), 2)

    def read(f, t, rows):
        return slab[f, t, rows, :] if f < 9 else (buo, lam, mu)[f - 9][t, rows, :]

    for out, lower in ((first, odd), (second, 1 - odd)):
        start = pl.multiple_of(lower * 8, 8)
        rows = pl.ds(start, 8)
        for i, (f, t) in enumerate(UP_PLANES):
            out[i] = read(f, t, rows)
        out[MISC - 1] = jnp.zeros((8, LANES), F32)
        for p, (f, t) in enumerate(REST):
            strip = jnp.where(lower == 1, read(f, t, slice(14, 16)), read(f, t, slice(0, 2)))
            out[STRIP + p // 4, 2 * (p % 4) : 2 * (p % 4) + 2, :] = strip
        out[MISC] = jnp.zeros((8, LANES), F32)
        for t in (0, 1):
            out[MISC, t : t + 1, :] = read(S12, t, slice(7, 8))
        out[MISC, 2:3, 0 : widths.shape[1]] = widths[...].astype(F32)
        for f in range(4):
            for k in range(4):
                cols = slice(k * LANES, (k + 1) * LANES)
                out[OCEAN + 4 * f + k] = ocean[f, rows, cols] if f < 3 else depth[rows, cols]


def sides(first, second):
    odd = lax.rem(lax.axis_index("sec"), 2)

    def top(i):
        return jnp.where(odd == 0, first[i], second[i])

    def bottom(i):
        return jnp.where(odd == 0, second[i], first[i])

    return top, bottom


def edges(x, r, tlane):
    out = None
    for t in range(DEPTH):
        moved = pltpu.roll(x[t, 8 * r : 8 * r + 8], (SPAN * t + 8) % LANES, 1)
        out = moved if t == 0 else jnp.where(tlane >= SPAN * t, moved, out)
    return out


def fill_strips(strips, first, second):
    top, bottom = sides(first, second)
    odd = lax.rem(lax.axis_index("sec"), 2)
    row = row_iota((8, LANES))
    for i, (f, t) in enumerate(UP_PLANES):
        strips[f, t] = jnp.where(row < 2, bottom(i), jnp.where(row >= 6, top(i), 0.0))
    for p, (f, t) in enumerate(REST):
        i, at = STRIP + p // 4, slice(2 * (p % 4), 2 * (p % 4) + 2)
        a, c = first[i, at, :], second[i, at, :]
        strips[f, t] = jnp.zeros((8, LANES), F32)
        strips[f, t, 0:2, :] = jnp.where(odd == 0, c, a)
        strips[f, t, 6:8, :] = jnp.where(odd == 0, a, c)


def halo_spot(i, tlane):
    at = 2 * (i % 8)
    spot = tlane % SPAN
    return i // 8, at, (spot >= at) & (spot < at + 2)


def carry_kernel(slab, buo, lam, mu, ocean, depth, state, sea, windows, halos):
    state[0:9] = slab[...]
    for i, x in enumerate((buo, lam, mu)):
        state[9 + i] = x[...]
    sea[0:3] = ocean[...]
    sea[3] = depth[...]
    tlane = lane_iota((8, LANES))
    heads = [jnp.zeros((8, LANES), F32) for _ in range(3)]
    tails = [jnp.zeros((8, LANES), F32) for _ in range(3)]
    for f in range(12):
        for r in range(2):
            x = edges(slab.at[f] if f < 9 else (buo, lam, mu)[f - 9], r, tlane)
            windows[f, 8 * r : 8 * r + 8, :] = x
            k, at, here = halo_spot(2 * f + r, tlane)
            heads[k] = jnp.where(here, pltpu.roll(x, (at - 8) % LANES, 1), heads[k])
            tails[k] = jnp.where(here, pltpu.roll(x, (at - 6) % LANES, 1), tails[k])
    for k in range(3):
        halos[0, k] = heads[k]
        halos[1, k] = tails[k]


def uplift_kernel(state, sea, halos, first, second, send, last, strips):
    me = lax.axis_index("blk")
    top, bottom = sides(first, second)
    shape = (32, LANES)
    lane, row = lane_iota(shape), row_iota(shape)

    def plane(f, t):
        i = UP_INDEX[(f, t)]
        return jnp.concatenate([top(i), state[f, t], bottom(i)], axis=0)

    def north(x):
        return pltpu.roll(x, 1, 0)

    def south(x):
        return pltpu.roll(x, 31, 0)

    def west(x):
        return jnp.where(lane == 0, 0.0, pltpu.roll(x, 1, 1))

    def east(x):
        return jnp.where(lane == LANES - 1, 0.0, pltpu.roll(x, LANES - 1, 1))

    s11 = [plane(S11, t) for t in range(3)]
    s22, s33, s23, s13, s12 = ([plane(f, t) for t in (0, 1)] for f in (S22, S33, S23, S13, S12))
    b, la, m = ([plane(f, t) for t in (0, 1)] for f in (BUO, LAM, MU))
    misc = top(MISC)
    v1, v2, v3 = [], [], []
    for t in (0, 1):
        above = lambda s: s[t] - s[t - 1] if t else s[t]
        s12n = jnp.where(row == 0, misc[t : t + 1, :], north(s12[t]))
        v1.append(plane(0, t) + Q * b[t] * (s11[t + 1] - s11[t] + (s12[t] - s12n) + (s13[t] - west(s13[t]))))
        v2.append(plane(1, t) + Q * b[t] * (south(s22[t]) - s22[t] + above(s12) + (s23[t] - west(s23[t]))))
        v3.append(plane(2, t) + Q * b[t] * (east(s33[t]) - s33[t] + above(s13) + (s23[t] - north(s23[t]))))
    n11 = []
    for t in (0, 1):
        d1 = v1[t] - v1[t - 1] if t else v1[t]
        dil = d1 + (v2[t] - north(v2[t])) + (v3[t] - west(v3[t]))
        n11.append(s11[t] + Q * (la[t] * dil + 2.0 * m[t] * d1))
    n12 = s12[0] + Q * m[0] * (south(v1[0]) - v1[0] + v2[1] - v2[0])
    n13 = s13[0] + Q * m[0] * (east(v1[0]) - v1[0] + v3[1] - v3[0])
    g = Q * Q * b[0]
    rise = 2.0 * Q * v1[0] + g * (n11[1] - n11[0] + n12 - north(n12) + n13 - west(n13))

    la0, la1 = Q * la[0], Q * la[1]
    m0, m1 = la0 + 2.0 * Q * m[0], la1 + 2.0 * Q * m[1]
    q0 = Q * m[0]
    q0n = north(q0)
    b0, b1 = Q * b[0], Q * b[1]
    left = [
        g * (la1 + q0) * b1,
        -g * (la0 + q0) * b0,
        g * q0,
        g * q0 * s13[0],
        s13[0],
        south(s13[0]),
        north(s13[0]),
        s13[1],
        s23[0],
        north(s23[0]),
        s23[1],
        north(s23[1]),
        v3[1],
        b1,
        v3[0],
        b0,
        n13,
        q0,
        q0 * s13[0],
        q0 * b1,
        q0 * b0,
        s13[0],
    ]
    right = [
        s33[1],
        s33[0],
        v1[0],
        -b0,
        -(2.0 * Q - g * (m1 + m0 + 2.0 * q0 + q0n)) * b0,
        -g * q0 * south(b0),
        -g * q0n * north(b0),
        -g * m1 * b1,
        g * (la0 + q0) * b0,
        -g * (la0 + q0n) * north(b0),
        -g * (la1 + q0) * b1,
        g * (la1 + q0n) * north(b1),
        -g * la1,
        -g * la1 * s33[1],
        g * la0,
        g * la0 * s33[0],
        -g,
        -g * v1[0],
        g * b0,
        -g * s33[1],
        g * s33[0],
        -pltpu.roll(g, LANES - 1, 1) * q0 * b0,
    ]
    factors = jnp.zeros(shape, F32)
    for i, (x, y) in enumerate(zip(left, right)):
        factors = jnp.where(lane == i, pltpu.roll(x, (i + 1) % LANES, 1), factors)
        factors = jnp.where(lane == 32 + i, pltpu.roll(y, 32 + i, 1), factors)
    packed = jnp.where(lane[:16] < 64, factors[:16], pltpu.roll(factors[16:], 64, 1))

    tile = (8, LANES)
    tlane = lane_iota(tile)
    fill_strips(strips, first, second)
    heads = [halos[0, k] for k in range(3)] + [jnp.zeros(tile, F32)]
    tails = [halos[1, k] for k in range(3)] + [jnp.zeros(tile, F32)]
    trow = row_iota(tile)
    empty = (trow >= 2) & (trow < 6)
    for p in range(6):
        pair = [edges(strips.at[2 * p + i], 0, tlane) for i in range(2)]
        for i in range(2):
            last[2 * p + i] = pair[i]
        x = jnp.where(empty, pltpu.roll(pair[1], 4, 0), pair[0])
        k, at, here = halo_spot(24 + p, tlane)
        heads[k] = jnp.where(here, pltpu.roll(x, (at - 8) % LANES, 1), heads[k])
        tails[k] = jnp.where(here, pltpu.roll(x, (at - 6) % LANES, 1), tails[k])
    head, tail = jnp.zeros(tile, F32), jnp.zeros(tile, F32)
    for f in range(4):
        for r in range(4):
            at = 32 * f + 8 * r
            ends = []
            for k in (0, 3):
                cols = slice(k * LANES, (k + 1) * LANES)
                rows = slice(8 * r - 8, 8 * r)
                if r == 0:
                    x = top(OCEAN + 4 * f + k)
                elif r == 3:
                    x = bottom(OCEAN + 4 * f + k)
                else:
                    x = sea[f, rows, cols]
                ends.append(x)
            here = (tlane >= at) & (tlane < at + 8)
            head = jnp.where(here, pltpu.roll(ends[0], at, 1), head)
            tail = jnp.where(here, pltpu.roll(ends[1], (at + 8) % LANES, 1), tail)
    heads.append(head)
    tails.append(tail)
    for d in range(send.shape[0]):
        for r in range(4):
            send[d, B_UP + r] = rise[8 * r : 8 * r + 8]
        for r in range(2):
            send[d, B_FACTOR + r] = packed[8 * r : 8 * r + 8]
        for i in range(5):
            send[d, B_SLAB + i] = jnp.where(d < me, heads[i], tails[i])


def filter_moves(source, target, sem):
    rows = [slice(k * LANES, (k + 1) * LANES + (16 if k == 3 else 0)) for k in range(4)]
    return [pltpu.make_async_copy(source.at[at, :], target.at[at, :], sem.at[k]) for k, at in enumerate(rows)]


def middle_kernel(
    state, sea, first, second, face, widths, plain_out, near, far, cells, mats, held, strips, plain, sem
):
    me = lax.axis_index("blk")
    top, bottom = sides(first, second)
    lane = lane_iota((1, LANES))
    face_at = (face[...] - me * COLS).astype(F32)
    width = face.shape[1]

    def scales(row):
        out = []
        for j in (me, me + 1, me - 1):
            w = jnp.sum(jnp.where(lane[:, : row.shape[1]] == j, row, 0.0), axis=1, keepdims=True)
            w = jnp.where(w > 0.0, w, 1.0)
            out.append((-(math.pi / 2.0) * math.log2(math.e) / w, 1.0 / w))
        return out

    groups = [scales(top(MISC)[2:3, :]), scales(widths[...].astype(F32)), scales(bottom(MISC)[2:3, :])]

    def put(k, rows, distance, rate, gain):
        decay = jnp.exp2(distance * rate)
        value = decay / (1.0 + decay * decay) * gain
        upper = value.astype(BF16)
        out, at = (near, 0) if k == 1 else (held, k * width)
        out[rows, at : at + width] = upper
        out[rows, at + width : at + 2 * width] = (value - upper.astype(F32)).astype(BF16)

    row = row_iota((16, width))
    at = jnp.where(row < 8, row + COLS, row - 16).astype(F32)
    distance = jnp.abs(at - face_at)
    for k in range(3):
        rate = jnp.where(row < 8, groups[k][1][0], groups[k][2][0])
        gain = jnp.where(row < 8, groups[k][1][1], groups[k][2][1])
        put(k, slice(COLS, COLS + 16), distance, rate, gain)
    moves = filter_moves(held, far, sem)
    for piece in range(4):

        @pl.loop(piece * LANES // 16, (piece + 1) * LANES // 16)
        def _(c):
            start = pl.multiple_of(c * 16, 16)
            at = (lax.broadcasted_iota(jnp.int32, (16, width), 0) + start).astype(F32)
            distance = jnp.abs(at - face_at)
            for k in range(3):
                put(k, pl.ds(start, 16), distance, *groups[k][0])

        moves[piece].start()

    for f in range(4):
        for k in range(4):
            cols = slice(k * LANES, (k + 1) * LANES)
            i = OCEAN + 4 * f + k
            plain[9 + f, 2 * k, 0:8, :] = top(i)
            plain[9 + f, 2 * k, 8:16, :] = sea[f, 0:8, cols]
            plain[9 + f, 2 * k + 1, 0:8, :] = sea[f, 8:16, cols]
            plain[9 + f, 2 * k + 1, 8:16, :] = bottom(i)

    fill_strips(strips, first, second)
    for f in range(9):
        for t in (0, DEPTH + 1):
            cells[f, t] = jnp.zeros((24, LANES), F32)
    for f in range(12):
        for t in range(DEPTH):
            if f < 9:
                cells[f, t + 1, 0:R, :] = state[f, t]
                cells[f, t + 1, R:, :] = strips[f, t]
            else:
                mats[f - 9, t, 0:R, :] = state[f, t]
                mats[f - 9, t, R:, :] = strips[f, t]
    north = lambda v: pltpu.roll(v, 1, 0)
    south = lambda v: pltpu.roll(v, 23, 0)
    west = lambda v: pltpu.roll(v, 1, 1)
    east = lambda v: pltpu.roll(v, LANES - 1, 1)
    for step in range(2):

        @pl.loop(1, DEPTH + 1)
        def _(t):
            s = [cells[3 + f, t] for f in range(6)]
            below, above = cells[S11, t + 1], (cells[S12, t - 1], cells[S13, t - 1])
            new = velocities([cells[a, t] for a in range(3)], s, Q * mats[0, t - 1], below, above, north, south, west, east)
            for a in range(3):
                cells[a, t] = new[a]

        @pl.loop(1, DEPTH + 1)
        def _(t):
            v = [cells[a, t] for a in range(3)]
            s = [cells[3 + f, t] for f in range(6)]
            below, above = (cells[1, t + 1], cells[2, t + 1]), cells[0, t - 1]
            new = stresses(s, v, Q * mats[1, t - 1], Q * mats[2, t - 1], below, above, north, south, west, east)
            if step == 0:
                for f in range(6):
                    cells[3 + f, t] = new[f]
            else:
                for f, x in enumerate(v + new):
                    plain[f, t - 1] = x[0:R]

    leave = pltpu.make_async_copy(plain, plain_out.at[0:13], sem.at[4])
    leave.start()
    for move in moves + [leave]:
        move.wait()


def velocities(v, s, qb, s11_below, above, north, south, west, east):
    s11, s22, s33, s23, s13, s12 = s
    return [
        v[0] + qb * (s11_below - s11 + (s12 - north(s12)) + (s13 - west(s13))),
        v[1] + qb * (south(s22) - s22 + (s12 - above[0]) + (s23 - west(s23))),
        v[2] + qb * (east(s33) - s33 + (s13 - above[1]) + (s23 - north(s23))),
    ]


def stresses(s, v, la, m, below, v1_above, north, south, west, east):
    v1, v2, v3 = v
    d1, d2, d3 = v1 - v1_above, v2 - north(v2), v3 - west(v3)
    dil = la * (d1 + d2 + d3)
    m2 = 2.0 * m
    return [
        s[0] + (dil + m2 * d1),
        s[1] + (dil + m2 * d2),
        s[2] + (dil + m2 * d3),
        s[3] + m * (east(v2) - v2 + (south(v3) - v3)),
        s[4] + m * (east(v1) - v1 + (below[1] - v3)),
        s[5] + m * (south(v1) - v1 + (below[0] - v2)),
    ]


def final_kernel(far, plain_in, near, windows, last, recv, slab_out, ocean_out, flat, held, plain, slab, sem):
    sec, me = lax.axis_index("sec"), lax.axis_index("blk")
    n_sec, n_blk = lax.axis_size("sec"), lax.axis_size("blk")
    shape = (32, LANES)
    lane, row = lane_iota(shape), row_iota(shape)
    before, after = jnp.maximum(me - 1, 0), jnp.minimum(me + 1, n_blk - 1)
    west_on, east_on = me > 0, me < n_blk - 1
    tile = (8, LANES)
    tlane = lane_iota(tile)

    enter = pltpu.make_async_copy(plain_in.at[0:13], plain, sem.at[5])
    moves = filter_moves(far, held, sem)
    for move in [enter] + moves:
        move.start()

    rises = [jnp.concatenate([recv[j, B_UP + r] for r in range(4)], axis=0) for j in range(n_blk)]
    factors = []
    for j in range(n_blk):
        x = jnp.concatenate([recv[j, B_FACTOR], recv[j, B_FACTOR + 1]], axis=0)
        factors.append(jnp.concatenate([x, pltpu.roll(x, 64, 1)], axis=0))
    for j in range(n_blk - 1):
        terms = factors[j] * pltpu.roll(factors[j + 1], LANES - 32, 1)
        pick = lambda a, z: jnp.sum(jnp.where((lane >= a) & (lane < z), terms, 0.0), axis=1, keepdims=True)
        rises[j] = rises[j] + jnp.where(lane == LANES - 1, pick(0, 4), 0.0)
        rises[j + 1] = rises[j + 1] + jnp.where(lane == 0, pick(4, 21), 0.0) + jnp.where(lane == 1, pick(21, 22), 0.0)
    rise = jnp.concatenate(rises, axis=1)
    rise_hi = rise.astype(BF16).astype(F32)
    rise_lo = rise - rise_hi
    wide = row_iota(rise.shape)
    upper = {}
    for k in (1, 0, 2):
        mine = (wide >= (0, 8, 24)[k]) & (wide < (8, 24, 32)[k])
        part = jnp.where(mine, rise_hi, 0.0)
        upper[k] = jnp.concatenate([part, jnp.where(mine, rise_lo, 0.0)], axis=0).astype(BF16)
        upper[k] = [upper[k], jnp.concatenate([part, jnp.zeros_like(part)], axis=0).astype(BF16)]

    def dot(a, c):
        return lax.dot_general(a, c, (((1,), (1,)), ((), ())), preferred_element_type=F32)

    for move in moves + [enter]:
        move.wait()
    source = dot(near[...], jnp.concatenate(upper[1], axis=1))
    source = source + dot(held[...], jnp.concatenate(upper[0] + upper[2], axis=1))
    flat[4 * LANES :, :] = jnp.zeros((LANES, LANES), F32)
    flat[0 : COLS + 8, 0:64] = source[0 : COLS + 8]
    flat[5 * LANES - 8 : 5 * LANES, 0:64] = source[COLS + 8 : COLS + 16]
    turned = [flat[k * LANES : (k + 1) * LANES, :].T for k in range(5)]
    source = jnp.concatenate([x[0:32] + x[32:64] for x in turned], axis=1)

    spot = tlane % SPAN
    north = lambda v: pltpu.roll(v, 1, 0)
    south = lambda v: pltpu.roll(v, 23, 0)
    west = lambda v: pltpu.roll(v, 1, 1)
    east = lambda v: pltpu.roll(v, LANES - 1, 1)
    wlane = lane_iota((24, LANES))
    above = lambda v: jnp.where(wlane < SPAN, 0.0, pltpu.roll(v, SPAN, 1))
    below = lambda v: jnp.where(wlane >= LANES - SPAN, 0.0, pltpu.roll(v, LANES - SPAN, 1))
    results = []
    for side in range(2):
        other, on, home = ((before, west_on, 6), (after, east_on, 8))[side]
        here = (spot >= home) & (spot < home + 2)
        state = []
        for f in range(12):
            parts = []
            for r in range(3):
                i = 2 * f + r if r < 2 else 24 + f // 2
                x = pltpu.roll(recv[other, B_SLAB + i // 8], (home - 2 * (i % 8)) % LANES, 1)
                if r == 2 and f % 2:
                    x = pltpu.roll(x, 4, 0)
                own = windows[f, 8 * r : 8 * r + 8, :] if r < 2 else last[f]
                parts.append(jnp.where(here, jnp.where(on, x, 0.0), own))
            state.append(jnp.concatenate(parts, axis=0))
        v, s = state[0:3], state[3:9]
        qb, la, m = Q * state[BUO], Q * state[LAM], Q * state[MU]
        for step in range(2):
            v = velocities(v, s, qb, below(s[0]), (above(s[5]), above(s[4])), north, south, west, east)
            s = stresses(s, v, la, m, (below(v[1]), below(v[2])), above(v[0]), north, south, west, east)
        results.append(v + s)
    edge = (tlane < 2) | (tlane >= LANES - 2)
    for f in range(9):
        for r in range(2):
            rows = slice(8 * r, 8 * r + 8)
            both = jnp.where(spot >= 8, results[0][f][rows], results[1][f][rows])
            for t in range(DEPTH):
                moved = pltpu.roll(both, (2 * LANES - SPAN * t - 8) % LANES, 1)
                slab[f, t, rows, :] = jnp.where(edge, moved, plain[f, t, rows, :])
    leave = pltpu.make_async_copy(slab, slab_out, sem.at[4])
    leave.start()

    ring = (32, 5 * LANES)
    fields = []
    for f in range(4):
        halo = []
        for r in range(4):
            at = 32 * f + 8 * r
            east_in = pltpu.roll(recv[after, B_OCEAN], (LANES - at) % LANES, 1)
            west_in = pltpu.roll(recv[before, B_OCEAN], (2 * LANES - 8 - at) % LANES, 1)
            x = jnp.where((tlane < 8) & east_on, east_in, 0.0)
            halo.append(jnp.where((tlane >= LANES - 8) & west_on, west_in, x))
        tiles = [jnp.concatenate([plain[9 + f, 2 * k], plain[9 + f, 2 * k + 1]], axis=0) for k in range(4)]
        fields.append(jnp.concatenate(tiles + [jnp.concatenate(halo, axis=0)], axis=1))
    surface, strike, dip, water = fields
    at = lane_iota(ring)
    at = jnp.where(at >= 5 * LANES - 8, at - 5 * LANES, at)
    x, y = row_iota(ring) - 8 + sec * R, at + me * COLS
    wet = (x >= 0) & (x < n_sec * R) & (y >= 0) & (y < n_blk * COLS) & (at < COLS + 8)
    surface = surface + source
    water = 0.25 * water
    for step in range(4):
        change = pltpu.roll(strike, 31, 0) - pltpu.roll(strike, 1, 0)
        change = change + (pltpu.roll(dip, 5 * LANES - 1, 1) - pltpu.roll(dip, 1, 1))
        surface = jnp.where(wet, surface - 0.25 * change, 0.0)
        strike = strike - water * (pltpu.roll(surface, 31, 0) - pltpu.roll(surface, 1, 0))
        dip = dip - water * (pltpu.roll(surface, 5 * LANES - 1, 1) - pltpu.roll(surface, 1, 1))
    ocean_out[0] = surface[8:24, 0:COLS]
    ocean_out[1] = strike[8:24, 0:COLS]
    ocean_out[2] = dip[8:24, 0:COLS]
    leave.wait()


def call(kernel, out_shape, flops, *args, far=0, out_far=(), limit=None, scratch=()):
    outs = list(out_shape)
    n_bytes = sum(a.size * a.dtype.itemsize for a in args) + sum(math.prod(o.shape) * o.dtype.itemsize for o in outs)
    anywhere = pl.BlockSpec(memory_space=pl.ANY)
    return pl.pallas_call(
        kernel,
        out_shape=out_shape,
        in_specs=[anywhere] * far + [VMEM] * (len(args) - far),
        out_specs=[anywhere if i in out_far else VMEM for i in range(len(outs))],
        scratch_shapes=scratch,
        compiler_params=pltpu.CompilerParams(vmem_limit_bytes=limit) if limit else None,
        cost_estimate=pl.CostEstimate(flops=flops, bytes_accessed=n_bytes, transcendentals=0),
    )(*args)


def swap(x, axis, start):
    pairs = []
    for i in range(start, lax.axis_size(axis) - 1, 2):
        pairs += [(i, i + 1), (i + 1, i)]
    return lax.ppermute(x, axis, pairs)


def on_device(slab_state, buoyancy, lame_lambda, lame_mu, face_map, band_widths, ocean_state, water_depth):
    n_blk = lax.axis_size("blk")
    n_face = face_map.shape[0]
    arr = jax.ShapeDtypeStruct
    own = (slab_state, buoyancy, lame_lambda, lame_mu, ocean_state, water_depth)
    message = arr((SEC_TILES, 8, LANES), F32)
    sources = (*own, band_widths)
    state, sea = arr((12, DEPTH, R, LANES), F32), arr((4, R, COLS), F32)
    first, second = call(
        pack_kernel,
        [message, message],
        10**6,
        *sources,
        far=7,
        scratch=[pltpu.VMEM(a.shape, a.dtype) for a in sources] + [pltpu.SemaphoreType.DMA((7,))],
    )
    first = swap(first, "sec", 1)
    second = swap(second, "sec", 0)
    state, sea, windows, halos = call(
        carry_kernel,
        [
            arr(state.shape, F32),
            arr(sea.shape, F32),
            arr((12, R, LANES), F32),
            arr((2, 3, 8, LANES), F32),
        ],
        10**7,
        *own,
        limit=MIB * 12,
    )
    strips = pltpu.VMEM((12, DEPTH, 8, LANES), F32)
    send, last = call(
        uplift_kernel,
        [arr((n_blk, BLK_TILES, 8, LANES), F32), arr((12, 8, LANES), F32)],
        10**7,
        state,
        sea,
        halos,
        first,
        second,
        limit=MIB * 12,
        scratch=[strips],
    )
    recv = lax.all_to_all(send, "blk", 0, 0, tiled=True)
    near = arr((COLS + 16, 2 * n_face), BF16)
    far = arr((6 * (COLS + 16), 4 * n_face), BF16)
    held = pltpu.VMEM((COLS + 16, 4 * n_face), BF16)
    plain = arr((PAD * 9, *slab_state.shape[1:]), F32)
    plain, near, far = call(
        middle_kernel,
        [plain, near, far],
        10**8,
        state,
        sea,
        first,
        second,
        face_map.reshape(1, n_face),
        band_widths,
        out_far=(0, 2),
        limit=MIB * 46,
        scratch=[
            pltpu.VMEM((9, DEPTH + 2, 24, LANES), F32),
            pltpu.VMEM((3, DEPTH, 24, LANES), F32),
            held,
            strips,
            pltpu.VMEM((13, DEPTH, R, LANES), F32),
            pltpu.SemaphoreType.DMA((5,)),
        ],
    )
    return call(
        final_kernel,
        [arr(slab_state.shape, F32), arr(ocean_state.shape, F32)],
        10**8,
        far,
        plain,
        near,
        windows,
        last,
        recv,
        far=2,
        out_far=(0,),
        limit=MIB * 46,
        scratch=[
            pltpu.VMEM((5 * LANES, LANES), F32),
            held,
            pltpu.VMEM((13, DEPTH, R, LANES), F32),
            pltpu.VMEM(slab_state.shape, F32),
            pltpu.SemaphoreType.DMA((6,)),
        ],
    )


def solution(mesh):
    in_specs = (
        P(None, None, "sec", "blk"),
        P(None, "sec", "blk"),
        P(None, "sec", "blk"),
        P(None, "sec", "blk"),
        P(),
        P("sec", None),
        P(None, "sec", "blk"),
        P("sec", "blk"),
    )
    out_specs = (P(None, None, "sec", "blk"), P(None, "sec", "blk"))
    return jax.shard_map(on_device, mesh=mesh, in_specs=in_specs, out_specs=out_specs, check_vma=False)
```

```python
import math

import jax
import jax.numpy as jnp
from jax import lax
from jax.experimental import pallas as pl
from jax.experimental.pallas import tpu as pltpu
from jax.sharding import PartitionSpec as P

Q = 0.25
R = 16
LANES = 128
DEPTH = 8
COLS = 512
S11, S22, S33, S23, S13, S12, BUO, LAM, MU = 3, 4, 5, 6, 7, 8, 9, 10, 11
UP_PLANES = [(S11, 0), (S11, 1), (S11, 2)] + [
    (f, t) for f in (S12, S13, S23, S22, S33, 0, 1, 2, BUO, LAM, MU) for t in (0, 1)
]
N_UP = len(UP_PLANES)
UP_INDEX = {ft: i for i, ft in enumerate(UP_PLANES)}
REST = [(f, t) for f in range(12) for t in range(DEPTH) if (f, t) not in UP_INDEX]
STRIP = N_UP
MISC = STRIP + (len(REST) + 3) // 4
OCEAN = MISC + 1
SEC_TILES = OCEAN + 16
B_UP, B_FACTOR, B_SLAB, B_OCEAN, BLK_TILES = 0, 4, 6, 10, 11
SPAN = 16
F32 = jnp.float32
MIB = 1 << 20
PAD = 36
BF16 = jnp.bfloat16
VMEM = pl.BlockSpec(memory_space=pltpu.VMEM)


def lane_iota(shape):
    return lax.broadcasted_iota(jnp.int32, shape, len(shape) - 1)


def row_iota(shape):
    return lax.broadcasted_iota(jnp.int32, shape, 0)


def fetch(sources, targets, sem):
    moves = [pltpu.make_async_copy(a, b, sem.at[i]) for i, (a, b) in enumerate(zip(sources, targets))]
    for move in moves:
        move.start()
    for move in moves:
        move.wait()


def pack_kernel(*refs):
    sources, (first, second), copies, sem = refs[:7], refs[7:9], refs[9:16], refs[16]
    fetch(sources, copies, sem)
    widths = copies[6]
    slab, buo, lam, mu, ocean, depth = copies[:6]
    odd = lax.rem(lax.axis_index("sec"), 2)

    def read(f, t, rows):
        return slab[f, t, rows, :] if f < 9 else (buo, lam, mu)[f - 9][t, rows, :]

    for out, lower in ((first, odd), (second, 1 - odd)):
        start = pl.multiple_of(lower * 8, 8)
        rows = pl.ds(start, 8)
        for i, (f, t) in enumerate(UP_PLANES):
            out[i] = read(f, t, rows)
        out[MISC - 1] = jnp.zeros((8, LANES), F32)
        for p, (f, t) in enumerate(REST):
            strip = jnp.where(lower == 1, read(f, t, slice(14, 16)), read(f, t, slice(0, 2)))
            out[STRIP + p // 4, 2 * (p % 4) : 2 * (p % 4) + 2, :] = strip
        out[MISC] = jnp.zeros((8, LANES), F32)
        for t in (0, 1):
            out[MISC, t : t + 1, :] = read(S12, t, slice(7, 8))
        out[MISC, 2:3, 0 : widths.shape[1]] = widths[...].astype(F32)
        for f in range(4):
            for k in range(4):
                cols = slice(k * LANES, (k + 1) * LANES)
                out[OCEAN + 4 * f + k] = ocean[f, rows, cols] if f < 3 else depth[rows, cols]


def sides(first, second):
    odd = lax.rem(lax.axis_index("sec"), 2)

    def top(i):
        return jnp.where(odd == 0, first[i], second[i])

    def bottom(i):
        return jnp.where(odd == 0, second[i], first[i])

    return top, bottom


def edges(x, r, tlane):
    out = None
    for t in range(DEPTH):
        moved = pltpu.roll(x[t, 8 * r : 8 * r + 8], (SPAN * t + 8) % LANES, 1)
        out = moved if t == 0 else jnp.where(tlane >= SPAN * t, moved, out)
    return out


def fill_strips(strips, first, second):
    top, bottom = sides(first, second)
    odd = lax.rem(lax.axis_index("sec"), 2)
    row = row_iota((8, LANES))
    for i, (f, t) in enumerate(UP_PLANES):
        strips[f, t] = jnp.where(row < 2, bottom(i), jnp.where(row >= 6, top(i), 0.0))
    for p, (f, t) in enumerate(REST):
        i, at = STRIP + p // 4, slice(2 * (p % 4), 2 * (p % 4) + 2)
        a, c = first[i, at, :], second[i, at, :]
        strips[f, t] = jnp.zeros((8, LANES), F32)
        strips[f, t, 0:2, :] = jnp.where(odd == 0, c, a)
        strips[f, t, 6:8, :] = jnp.where(odd == 0, a, c)


def halo_spot(i, tlane):
    at = 2 * (i % 8)
    spot = tlane % SPAN
    return i // 8, at, (spot >= at) & (spot < at + 2)


def carry_kernel(slab, buo, lam, mu, ocean, depth, state, sea, windows, halos):
    state[0:9] = slab[...]
    for i, x in enumerate((buo, lam, mu)):
        state[9 + i] = x[...]
    sea[0:3] = ocean[...]
    sea[3] = depth[...]
    tlane = lane_iota((8, LANES))
    heads = [jnp.zeros((8, LANES), F32) for _ in range(3)]
    tails = [jnp.zeros((8, LANES), F32) for _ in range(3)]
    for f in range(12):
        for r in range(2):
            x = edges(slab.at[f] if f < 9 else (buo, lam, mu)[f - 9], r, tlane)
            windows[f, 8 * r : 8 * r + 8, :] = x
            k, at, here = halo_spot(2 * f + r, tlane)
            heads[k] = jnp.where(here, pltpu.roll(x, (at - 8) % LANES, 1), heads[k])
            tails[k] = jnp.where(here, pltpu.roll(x, (at - 6) % LANES, 1), tails[k])
    for k in range(3):
        halos[0, k] = heads[k]
        halos[1, k] = tails[k]


def uplift_kernel(state, sea, halos, first, second, send, last, strips):
    me = lax.axis_index("blk")
    top, bottom = sides(first, second)
    shape = (32, LANES)
    lane, row = lane_iota(shape), row_iota(shape)

    def plane(f, t):
        i = UP_INDEX[(f, t)]
        return jnp.concatenate([top(i), state[f, t], bottom(i)], axis=0)

    def north(x):
        return pltpu.roll(x, 1, 0)

    def south(x):
        return pltpu.roll(x, 31, 0)

    def west(x):
        return jnp.where(lane == 0, 0.0, pltpu.roll(x, 1, 1))

    def east(x):
        return jnp.where(lane == LANES - 1, 0.0, pltpu.roll(x, LANES - 1, 1))

    s11 = [plane(S11, t) for t in range(3)]
    s22, s33, s23, s13, s12 = ([plane(f, t) for t in (0, 1)] for f in (S22, S33, S23, S13, S12))
    b, la, m = ([plane(f, t) for t in (0, 1)] for f in (BUO, LAM, MU))
    misc = top(MISC)
    v1, v2, v3 = [], [], []
    for t in (0, 1):
        above = lambda s: s[t] - s[t - 1] if t else s[t]
        s12n = jnp.where(row == 0, misc[t : t + 1, :], north(s12[t]))
        v1.append(plane(0, t) + Q * b[t] * (s11[t + 1] - s11[t] + (s12[t] - s12n) + (s13[t] - west(s13[t]))))
        v2.append(plane(1, t) + Q * b[t] * (south(s22[t]) - s22[t] + above(s12) + (s23[t] - west(s23[t]))))
        v3.append(plane(2, t) + Q * b[t] * (east(s33[t]) - s33[t] + above(s13) + (s23[t] - north(s23[t]))))
    n11 = []
    for t in (0, 1):
        d1 = v1[t] - v1[t - 1] if t else v1[t]
        dil = d1 + (v2[t] - north(v2[t])) + (v3[t] - west(v3[t]))
        n11.append(s11[t] + Q * (la[t] * dil + 2.0 * m[t] * d1))
    n12 = s12[0] + Q * m[0] * (south(v1[0]) - v1[0] + v2[1] - v2[0])
    n13 = s13[0] + Q * m[0] * (east(v1[0]) - v1[0] + v3[1] - v3[0])
    g = Q * Q * b[0]
    rise = 2.0 * Q * v1[0] + g * (n11[1] - n11[0] + n12 - north(n12) + n13 - west(n13))

    la0, la1 = Q * la[0], Q * la[1]
    m0, m1 = la0 + 2.0 * Q * m[0], la1 + 2.0 * Q * m[1]
    q0 = Q * m[0]
    q0n = north(q0)
    b0, b1 = Q * b[0], Q * b[1]
    left = [
        g * (la1 + q0) * b1,
        -g * (la0 + q0) * b0,
        g * q0,
        g * q0 * s13[0],
        s13[0],
        south(s13[0]),
        north(s13[0]),
        s13[1],
        s23[0],
        north(s23[0]),
        s23[1],
        north(s23[1]),
        v3[1],
        b1,
        v3[0],
        b0,
        n13,
        q0,
        q0 * s13[0],
        q0 * b1,
        q0 * b0,
        s13[0],
    ]
    right = [
        s33[1],
        s33[0],
        v1[0],
        -b0,
        -(2.0 * Q - g * (m1 + m0 + 2.0 * q0 + q0n)) * b0,
        -g * q0 * south(b0),
        -g * q0n * north(b0),
        -g * m1 * b1,
        g * (la0 + q0) * b0,
        -g * (la0 + q0n) * north(b0),
        -g * (la1 + q0) * b1,
        g * (la1 + q0n) * north(b1),
        -g * la1,
        -g * la1 * s33[1],
        g * la0,
        g * la0 * s33[0],
        -g,
        -g * v1[0],
        g * b0,
        -g * s33[1],
        g * s33[0],
        -pltpu.roll(g, LANES - 1, 1) * q0 * b0,
    ]
    factors = jnp.zeros(shape, F32)
    for i, (x, y) in enumerate(zip(left, right)):
        factors = jnp.where(lane == i, pltpu.roll(x, (i + 1) % LANES, 1), factors)
        factors = jnp.where(lane == 32 + i, pltpu.roll(y, 32 + i, 1), factors)
    packed = jnp.where(lane[:16] < 64, factors[:16], pltpu.roll(factors[16:], 64, 1))

    tile = (8, LANES)
    tlane = lane_iota(tile)
    fill_strips(strips, first, second)
    heads = [halos[0, k] for k in range(3)] + [jnp.zeros(tile, F32)]
    tails = [halos[1, k] for k in range(3)] + [jnp.zeros(tile, F32)]
    trow = row_iota(tile)
    empty = (trow >= 2) & (trow < 6)
    for p in range(6):
        pair = [edges(strips.at[2 * p + i], 0, tlane) for i in range(2)]
        for i in range(2):
            last[2 * p + i] = pair[i]
        x = jnp.where(empty, pltpu.roll(pair[1], 4, 0), pair[0])
        k, at, here = halo_spot(24 + p, tlane)
        heads[k] = jnp.where(here, pltpu.roll(x, (at - 8) % LANES, 1), heads[k])
        tails[k] = jnp.where(here, pltpu.roll(x, (at - 6) % LANES, 1), tails[k])
    head, tail = jnp.zeros(tile, F32), jnp.zeros(tile, F32)
    for f in range(4):
        for r in range(4):
            at = 32 * f + 8 * r
            ends = []
            for k in (0, 3):
                cols = slice(k * LANES, (k + 1) * LANES)
                rows = slice(8 * r - 8, 8 * r)
                if r == 0:
                    x = top(OCEAN + 4 * f + k)
                elif r == 3:
                    x = bottom(OCEAN + 4 * f + k)
                else:
                    x = sea[f, rows, cols]
                ends.append(x)
            here = (tlane >= at) & (tlane < at + 8)
            head = jnp.where(here, pltpu.roll(ends[0], at, 1), head)
            tail = jnp.where(here, pltpu.roll(ends[1], (at + 8) % LANES, 1), tail)
    heads.append(head)
    tails.append(tail)
    for d in range(send.shape[0]):
        for r in range(4):
            send[d, B_UP + r] = rise[8 * r : 8 * r + 8]
        for r in range(2):
            send[d, B_FACTOR + r] = packed[8 * r : 8 * r + 8]
        for i in range(5):
            send[d, B_SLAB + i] = jnp.where(d < me, heads[i], tails[i])


def filter_moves(source, target, sem):
    rows = [slice(k * LANES, (k + 1) * LANES + (16 if k == 3 else 0)) for k in range(4)]
    return [pltpu.make_async_copy(source.at[at, :], target.at[at, :], sem.at[k]) for k, at in enumerate(rows)]


def middle_kernel(
    state, sea, first, second, face, widths, plain_out, near, far, cells, mats, held, strips, plain, sem
):
    me = lax.axis_index("blk")
    top, bottom = sides(first, second)
    lane = lane_iota((1, LANES))
    face_at = (face[...] - me * COLS).astype(F32)
    width = face.shape[1]

    def scales(row):
        out = []
        for j in (me, me + 1, me - 1):
            w = jnp.sum(jnp.where(lane[:, : row.shape[1]] == j, row, 0.0), axis=1, keepdims=True)
            w = jnp.where(w > 0.0, w, 1.0)
            out.append((-(math.pi / 2.0) * math.log2(math.e) / w, 1.0 / w))
        return out

    groups = [scales(top(MISC)[2:3, :]), scales(widths[...].astype(F32)), scales(bottom(MISC)[2:3, :])]

    def put(k, rows, distance, rate, gain):
        decay = jnp.exp2(distance * rate)
        value = decay / (1.0 + decay * decay) * gain
        upper = value.astype(BF16)
        out, at = (near, 0) if k == 1 else (held, k * width)
        out[rows, at : at + width] = upper
        out[rows, at + width : at + 2 * width] = (value - upper.astype(F32)).astype(BF16)

    row = row_iota((16, width))
    at = jnp.where(row < 8, row + COLS, row - 16).astype(F32)
    distance = jnp.abs(at - face_at)
    for k in range(3):
        rate = jnp.where(row < 8, groups[k][1][0], groups[k][2][0])
        gain = jnp.where(row < 8, groups[k][1][1], groups[k][2][1])
        put(k, slice(COLS, COLS + 16), distance, rate, gain)
    moves = filter_moves(held, far, sem)
    for piece in range(4):

        @pl.loop(piece * LANES // 16, (piece + 1) * LANES // 16)
        def _(c):
            start = pl.multiple_of(c * 16, 16)
            at = (lax.broadcasted_iota(jnp.int32, (16, width), 0) + start).astype(F32)
            distance = jnp.abs(at - face_at)
            for k in range(3):
                put(k, pl.ds(start, 16), distance, *groups[k][0])

        moves[piece].start()

    for f in range(4):
        for k in range(4):
            cols = slice(k * LANES, (k + 1) * LANES)
            i = OCEAN + 4 * f + k
            plain[9 + f, 2 * k, 0:8, :] = top(i)
            plain[9 + f, 2 * k, 8:16, :] = sea[f, 0:8, cols]
            plain[9 + f, 2 * k + 1, 0:8, :] = sea[f, 8:16, cols]
            plain[9 + f, 2 * k + 1, 8:16, :] = bottom(i)

    fill_strips(strips, first, second)
    for f in range(9):
        for t in (0, DEPTH + 1):
            cells[f, t] = jnp.zeros((24, LANES), F32)
    for f in range(12):
        for t in range(DEPTH):
            if f < 9:
                cells[f, t + 1, 0:R, :] = state[f, t]
                cells[f, t + 1, R:, :] = strips[f, t]
            else:
                mats[f - 9, t, 0:R, :] = state[f, t]
                mats[f - 9, t, R:, :] = strips[f, t]
    north = lambda v: pltpu.roll(v, 1, 0)
    south = lambda v: pltpu.roll(v, 23, 0)
    west = lambda v: pltpu.roll(v, 1, 1)
    east = lambda v: pltpu.roll(v, LANES - 1, 1)
    for step in range(2):

        @pl.loop(1, DEPTH + 1)
        def _(t):
            s = [cells[3 + f, t] for f in range(6)]
            below, above = cells[S11, t + 1], (cells[S12, t - 1], cells[S13, t - 1])
            new = velocities([cells[a, t] for a in range(3)], s, Q * mats[0, t - 1], below, above, north, south, west, east)
            for a in range(3):
                cells[a, t] = new[a]

        @pl.loop(1, DEPTH + 1)
        def _(t):
            v = [cells[a, t] for a in range(3)]
            s = [cells[3 + f, t] for f in range(6)]
            below, above = (cells[1, t + 1], cells[2, t + 1]), cells[0, t - 1]
            new = stresses(s, v, Q * mats[1, t - 1], Q * mats[2, t - 1], below, above, north, south, west, east)
            if step == 0:
                for f in range(6):
                    cells[3 + f, t] = new[f]
            else:
                for f, x in enumerate(v + new):
                    plain[f, t - 1] = x[0:R]

    leave = pltpu.make_async_copy(plain, plain_out.at[0:13], sem.at[4])
    leave.start()
    for move in moves + [leave]:
        move.wait()


def velocities(v, s, qb, s11_below, above, north, south, west, east):
    s11, s22, s33, s23, s13, s12 = s
    return [
        v[0] + qb * (s11_below - s11 + (s12 - north(s12)) + (s13 - west(s13))),
        v[1] + qb * (south(s22) - s22 + (s12 - above[0]) + (s23 - west(s23))),
        v[2] + qb * (east(s33) - s33 + (s13 - above[1]) + (s23 - north(s23))),
    ]


def stresses(s, v, la, m, below, v1_above, north, south, west, east):
    v1, v2, v3 = v
    d1, d2, d3 = v1 - v1_above, v2 - north(v2), v3 - west(v3)
    dil = la * (d1 + d2 + d3)
    m2 = 2.0 * m
    return [
        s[0] + (dil + m2 * d1),
        s[1] + (dil + m2 * d2),
        s[2] + (dil + m2 * d3),
        s[3] + m * (east(v2) - v2 + (south(v3) - v3)),
        s[4] + m * (east(v1) - v1 + (below[1] - v3)),
        s[5] + m * (south(v1) - v1 + (below[0] - v2)),
    ]


def final_kernel(far, plain_in, near, windows, last, recv, slab_out, ocean_out, flat, held, plain, slab, sem):
    sec, me = lax.axis_index("sec"), lax.axis_index("blk")
    n_sec, n_blk = lax.axis_size("sec"), lax.axis_size("blk")
    shape = (32, LANES)
    lane, row = lane_iota(shape), row_iota(shape)
    before, after = jnp.maximum(me - 1, 0), jnp.minimum(me + 1, n_blk - 1)
    west_on, east_on = me > 0, me < n_blk - 1
    tile = (8, LANES)
    tlane = lane_iota(tile)

    enter = pltpu.make_async_copy(plain_in.at[0:13], plain, sem.at[5])
    moves = [pltpu.make_async_copy(far.at[0 : COLS + 16, :], held, sem.at[0])]
    for move in [enter] + moves:
        move.start()

    rises = [jnp.concatenate([recv[j, B_UP + r] for r in range(4)], axis=0) for j in range(n_blk)]
    factors = []
    for j in range(n_blk):
        x = jnp.concatenate([recv[j, B_FACTOR], recv[j, B_FACTOR + 1]], axis=0)
        factors.append(jnp.concatenate([x, pltpu.roll(x, 64, 1)], axis=0))
    for j in range(n_blk - 1):
        terms = factors[j] * pltpu.roll(factors[j + 1], LANES - 32, 1)
        pick = lambda a, z: jnp.sum(jnp.where((lane >= a) & (lane < z), terms, 0.0), axis=1, keepdims=True)
        rises[j] = rises[j] + jnp.where(lane == LANES - 1, pick(0, 4), 0.0)
        rises[j + 1] = rises[j + 1] + jnp.where(lane == 0, pick(4, 21), 0.0) + jnp.where(lane == 1, pick(21, 22), 0.0)
    rise = jnp.concatenate(rises, axis=1)
    rise_hi = rise.astype(BF16).astype(F32)
    rise_lo = rise - rise_hi
    wide = row_iota(rise.shape)
    upper = {}
    for k in (1, 0, 2):
        mine = (wide >= (0, 8, 24)[k]) & (wide < (8, 24, 32)[k])
        part = jnp.where(mine, rise_hi, 0.0)
        upper[k] = jnp.concatenate([part, jnp.where(mine, rise_lo, 0.0)], axis=0).astype(BF16)
        upper[k] = [upper[k], jnp.concatenate([part, jnp.zeros_like(part)], axis=0).astype(BF16)]

    def dot(a, c):
        return lax.dot_general(a, c, (((1,), (1,)), ((), ())), preferred_element_type=F32)

    for move in moves + [enter]:
        move.wait()
    source = dot(near[...], jnp.concatenate(upper[1], axis=1))
    source = source + dot(held[...], jnp.concatenate(upper[0] + upper[2], axis=1))
    flat[4 * LANES :, :] = jnp.zeros((LANES, LANES), F32)
    flat[0 : COLS + 8, 0:64] = source[0 : COLS + 8]
    flat[5 * LANES - 8 : 5 * LANES, 0:64] = source[COLS + 8 : COLS + 16]
    turned = [flat[k * LANES : (k + 1) * LANES, :].T for k in range(5)]
    source = jnp.concatenate([x[0:32] + x[32:64] for x in turned], axis=1)

    spot = tlane % SPAN
    north = lambda v: pltpu.roll(v, 1, 0)
    south = lambda v: pltpu.roll(v, 23, 0)
    west = lambda v: pltpu.roll(v, 1, 1)
    east = lambda v: pltpu.roll(v, LANES - 1, 1)
    wlane = lane_iota((24, LANES))
    above = lambda v: jnp.where(wlane < SPAN, 0.0, pltpu.roll(v, SPAN, 1))
    below = lambda v: jnp.where(wlane >= LANES - SPAN, 0.0, pltpu.roll(v, LANES - SPAN, 1))
    results = []
    for side in range(2):
        other, on, home = ((before, west_on, 6), (after, east_on, 8))[side]
        here = (spot >= home) & (spot < home + 2)
        state = []
        for f in range(12):
            parts = []
            for r in range(3):
                i = 2 * f + r if r < 2 else 24 + f // 2
                x = pltpu.roll(recv[other, B_SLAB + i // 8], (home - 2 * (i % 8)) % LANES, 1)
                if r == 2 and f % 2:
                    x = pltpu.roll(x, 4, 0)
                own = windows[f, 8 * r : 8 * r + 8, :] if r < 2 else last[f]
                parts.append(jnp.where(here, jnp.where(on, x, 0.0), own))
            state.append(jnp.concatenate(parts, axis=0))
        v, s = state[0:3], state[3:9]
        qb, la, m = Q * state[BUO], Q * state[LAM], Q * state[MU]
        for step in range(2):
            v = velocities(v, s, qb, below(s[0]), (above(s[5]), above(s[4])), north, south, west, east)
            s = stresses(s, v, la, m, (below(v[1]), below(v[2])), above(v[0]), north, south, west, east)
        results.append(v + s)
    edge = (tlane < 2) | (tlane >= LANES - 2)
    for f in range(9):
        for r in range(2):
            rows = slice(8 * r, 8 * r + 8)
            both = jnp.where(spot >= 8, results[0][f][rows], results[1][f][rows])
            for t in range(DEPTH):
                moved = pltpu.roll(both, (2 * LANES - SPAN * t - 8) % LANES, 1)
                slab[f, t, rows, :] = jnp.where(edge, moved, plain[f, t, rows, :])
    leave = pltpu.make_async_copy(slab, slab_out, sem.at[4])
    leave.start()

    ring = (32, 5 * LANES)
    fields = []
    for f in range(4):
        halo = []
        for r in range(4):
            at = 32 * f + 8 * r
            east_in = pltpu.roll(recv[after, B_OCEAN], (LANES - at) % LANES, 1)
            west_in = pltpu.roll(recv[before, B_OCEAN], (2 * LANES - 8 - at) % LANES, 1)
            x = jnp.where((tlane < 8) & east_on, east_in, 0.0)
            halo.append(jnp.where((tlane >= LANES - 8) & west_on, west_in, x))
        tiles = [jnp.concatenate([plain[9 + f, 2 * k], plain[9 + f, 2 * k + 1]], axis=0) for k in range(4)]
        fields.append(jnp.concatenate(tiles + [jnp.concatenate(halo, axis=0)], axis=1))
    surface, strike, dip, water = fields
    at = lane_iota(ring)
    at = jnp.where(at >= 5 * LANES - 8, at - 5 * LANES, at)
    x, y = row_iota(ring) - 8 + sec * R, at + me * COLS
    wet = (x >= 0) & (x < n_sec * R) & (y >= 0) & (y < n_blk * COLS) & (at < COLS + 8)
    surface = surface + source
    water = 0.25 * water
    for step in range(4):
        change = pltpu.roll(strike, 31, 0) - pltpu.roll(strike, 1, 0)
        change = change + (pltpu.roll(dip, 5 * LANES - 1, 1) - pltpu.roll(dip, 1, 1))
        surface = jnp.where(wet, surface - 0.25 * change, 0.0)
        strike = strike - water * (pltpu.roll(surface, 31, 0) - pltpu.roll(surface, 1, 0))
        dip = dip - water * (pltpu.roll(surface, 5 * LANES - 1, 1) - pltpu.roll(surface, 1, 1))
    ocean_out[0] = surface[8:24, 0:COLS]
    ocean_out[1] = strike[8:24, 0:COLS]
    ocean_out[2] = dip[8:24, 0:COLS]
    leave.wait()


def call(kernel, out_shape, flops, *args, far=0, out_far=(), limit=None, scratch=()):
    outs = list(out_shape)
    n_bytes = sum(a.size * a.dtype.itemsize for a in args) + sum(math.prod(o.shape) * o.dtype.itemsize for o in outs)
    anywhere = pl.BlockSpec(memory_space=pl.ANY)
    return pl.pallas_call(
        kernel,
        out_shape=out_shape,
        in_specs=[anywhere] * far + [VMEM] * (len(args) - far),
        out_specs=[anywhere if i in out_far else VMEM for i in range(len(outs))],
        scratch_shapes=scratch,
        compiler_params=pltpu.CompilerParams(vmem_limit_bytes=limit) if limit else None,
        cost_estimate=pl.CostEstimate(flops=flops, bytes_accessed=n_bytes, transcendentals=0),
    )(*args)


def swap(x, axis, start):
    pairs = []
    for i in range(start, lax.axis_size(axis) - 1, 2):
        pairs += [(i, i + 1), (i + 1, i)]
    return lax.ppermute(x, axis, pairs)


def on_device(slab_state, buoyancy, lame_lambda, lame_mu, face_map, band_widths, ocean_state, water_depth):
    n_blk = lax.axis_size("blk")
    n_face = face_map.shape[0]
    arr = jax.ShapeDtypeStruct
    own = (slab_state, buoyancy, lame_lambda, lame_mu, ocean_state, water_depth)
    message = arr((SEC_TILES, 8, LANES), F32)
    sources = (*own, band_widths)
    state, sea = arr((12, DEPTH, R, LANES), F32), arr((4, R, COLS), F32)
    first, second = call(
        pack_kernel,
        [message, message],
        10**6,
        *sources,
        far=7,
        scratch=[pltpu.VMEM(a.shape, a.dtype) for a in sources] + [pltpu.SemaphoreType.DMA((7,))],
    )
    first = swap(first, "sec", 1)
    second = swap(second, "sec", 0)
    state, sea, windows, halos = call(
        carry_kernel,
        [
            arr(state.shape, F32),
            arr(sea.shape, F32),
            arr((12, R, LANES), F32),
            arr((2, 3, 8, LANES), F32),
        ],
        10**7,
        *own,
        limit=MIB * 12,
    )
    strips = pltpu.VMEM((12, DEPTH, 8, LANES), F32)
    send, last = call(
        uplift_kernel,
        [arr((n_blk, BLK_TILES, 8, LANES), F32), arr((12, 8, LANES), F32)],
        10**7,
        state,
        sea,
        halos,
        first,
        second,
        limit=MIB * 12,
        scratch=[strips],
    )
    recv = lax.all_to_all(send, "blk", 0, 0, tiled=True)
    near = arr((COLS + 16, 2 * n_face), BF16)
    far = arr((6 * (COLS + 16), 4 * n_face), BF16)
    held = pltpu.VMEM((COLS + 16, 4 * n_face), BF16)
    plain = arr((PAD * 9, *slab_state.shape[1:]), F32)
    plain, near, far = call(
        middle_kernel,
        [plain, near, far],
        10**8,
        state,
        sea,
        first,
        second,
        face_map.reshape(1, n_face),
        band_widths,
        out_far=(0, 2),
        limit=MIB * 46,
        scratch=[
            pltpu.VMEM((9, DEPTH + 2, 24, LANES), F32),
            pltpu.VMEM((3, DEPTH, 24, LANES), F32),
            held,
            strips,
            pltpu.VMEM((13, DEPTH, R, LANES), F32),
            pltpu.SemaphoreType.DMA((5,)),
        ],
    )
    return call(
        final_kernel,
        [arr(slab_state.shape, F32), arr(ocean_state.shape, F32)],
        10**8,
        far,
        plain,
        near,
        windows,
        last,
        recv,
        far=2,
        out_far=(0,),
        limit=MIB * 46,
        scratch=[
            pltpu.VMEM((5 * LANES, LANES), F32),
            held,
            pltpu.VMEM((13, DEPTH, R, LANES), F32),
            pltpu.VMEM(slab_state.shape, F32),
            pltpu.SemaphoreType.DMA((6,)),
        ],
    )


def solution(mesh):
    in_specs = (
        P(None, None, "sec", "blk"),
        P(None, "sec", "blk"),
        P(None, "sec", "blk"),
        P(None, "sec", "blk"),
        P(),
        P("sec", None),
        P(None, "sec", "blk"),
        P("sec", "blk"),
    )
    out_specs = (P(None, None, "sec", "blk"), P(None, "sec", "blk"))
    return jax.shard_map(on_device, mesh=mesh, in_specs=in_specs, out_specs=out_specs, check_vma=False)
```
